32 devices in a mesh: dp: 8 (over z, x), tensor: 4 (over y, core).
Axes of the slice: x: 2, y: 2, z: 4, core: 2. Of those that a mesh axis runs over, the one named last changes fastest.
Arguments:
- images: bfloat16 [16, 196, 768], P('dp'), may hold values from -6 to 6
- mask_places: int32 [16, 80], P('dp'), may hold values from 0 to 195, as said below
- mask_counts: int32 [16], replicated, may hold values from 60 to 80, as said below
- codes: int32 [16, 196], P('dp'), may hold values from 0 to 8191
- step_count: int32 [1], replicated, may hold values from 1 to 20
- in_weights: float32 [1, 768, 7, 768], P(None, 'dp', None, 'tensor'), may hold values from -0.21875 to 0.21875
- in_moments: float32 [2, 1, 768, 7, 768], P(None, None, 'dp', None, 'tensor'), may hold values from -1 to 1, as said below
- out_weights: float32 [1, 5, 768, 768], P(None, None, 'tensor', 'dp'), may hold values from -1.5 to 1.5
- out_moments: float32 [2, 1, 5, 768, 768], P(None, None, None, 'tensor', 'dp'), may hold values from -1 to 1, as said below
- patch_weight: float32 [768, 768], P('dp'), may hold values from -0.21875 to 0.21875
- patch_moments: float32 [2, 768, 768], P(None, 'dp'), may hold values from -1 to 1, as said below
- code_weight: float32 [768, 8192], P('dp', 'tensor'), may hold values from -0.4375 to 0.4375
- code_moments: float32 [2, 768, 8192], P(None, 'dp', 'tensor'), may hold values from -1 to 1, as said below
- in_biases: float32 [1, 6, 768], P(None, None, 'tensor'), may hold values from -4 to 4
- bias_moments: float32 [2, 1, 6, 768], P(None, None, None, 'tensor'), may hold values from -1 to 1, as said below
- vectors: float32 [13, 768], replicated, may hold values from -4 to 4, as said below
- vector_moments: float32 [2, 13, 768], replicated, may hold values from -1 to 1, as said below
- rel_table: float32 [12, 732], P('tensor'), may hold values from -6 to 6
- table_moments: float32 [2, 12, 732], P(None, 'tensor'), may hold values from -1 to 1, as said below
- logit_bias: float32 [8192], P('tensor'), may hold values from -6 to 6
- logit_moments: float32 [2, 8192], P(None, 'tensor'), may hold values from -1 to 1, as said below
Outputs:
- loss_value: float32 [1], replicated
- grad_norm: float32 [1], replicated
- in_master: float32 [1, 768, 7, 768], P(None, 'dp', None, 'tensor')
- in_state: float32 [2, 1, 768, 7, 768], P(None, None, 'dp', None, 'tensor')
- out_master: float32 [1, 5, 768, 768], P(None, None, 'tensor', 'dp')
- out_state: float32 [2, 1, 5, 768, 768], P(None, None, None, 'tensor', 'dp')
- patch_master: float32 [768, 768], P('dp')
- patch_state: float32 [2, 768, 768], P(None, 'dp')
- code_master: float32 [768, 8192], P('dp', 'tensor')
- code_state: float32 [2, 768, 8192], P(None, 'dp', 'tensor')
- bias_master: float32 [1, 6, 768], P(None, None, 'tensor')
- bias_state: float32 [2, 1, 6, 768], P(None, None, None, 'tensor')
- vector_master: float32 [13, 768], replicated
- vector_state: float32 [2, 13, 768], replicated
- table_master: float32 [12, 732], P('tensor')
- table_state: float32 [2, 12, 732], P(None, 'tensor')
- logit_master: float32 [8192], P('tensor')
- logit_state: float32 [2, 8192], P(None, 'tensor')
The draws below stay inside these ranges and needn't reach their ends.
Inputs may be any that keep to these rules, and one draw needn't show every extreme that they name: `mask_places`: each row names 80 different patches; entries past the image's count are ignored. `mask_counts`: some image has exactly 80 valid entries. `vectors`: Layer-scale rows are positive. `in_moments`: the second rows are positive. `out_moments`: the second rows are positive. `patch_moments`: the second rows are positive. `code_moments`: the second rows are positive. `bias_moments`: the second rows are positive. `vector_moments`: the second rows are positive. `table_moments`: the second rows are positive. `logit_moments`: the second rows are positive.
All inputs are finite; a program needn't handle non-finite values.
Results may differ from the reference program's by a relative error of at most 0.012.
The reference program's roundings to bfloat16 on the way count: a program that leaves them out, or rounds other values in their place, can miss the bound.
Values may be sent and summed in bfloat16 or wider, within the bound.
No kernel may reach another device: no remote copies, remote signals or barrier semaphores. Data moves between devices by JAX's collectives and lax.ppermute only.
A program may use at most 128 MiB of HBM per device.

```python
import jax
import jax.numpy as jnp
from jax import lax

D = 768
H = 12
HD = 64
FF = 3072
V = 8192
P_SIZE = 768
GRID = 14
L = 1
MB = 2
MASK = 80
IMG_MB = 1
NPATCH = 196
SEQ = 197
NREL = 732
IMAGES = 16
N_TENSOR = 4


def draw_mask_places(key, part):
    keys = jax.random.split(key, IMAGES)
    return jax.vmap(lambda k: jax.random.permutation(k, NPATCH)[:MASK])(keys).astype(jnp.int32)


def draw_mask_counts(key, part):
    drawn = jax.random.randint(key, (IMAGES,), 3 * MASK // 4, MASK + 1, dtype=jnp.int32)
    return drawn.at[0].set(MASK).astype(jnp.int32)


def draw_out_weights(key, part):
    normal_draw = jnp.clip(jax.random.normal(key, (L, 5, D, D), jnp.float32), -4.0, 4.0)
    blocks = jnp.arange(5, dtype=jnp.int32)[None, :, None, None]
    scales = jnp.where(blocks == 0, (8.0 / D) ** 0.5, (1.0 / FF) ** 0.5)
    return normal_draw * scales


def draw_vectors(key, part):
    row_total = 8 * L + 5
    row_kinds = jnp.arange(row_total, dtype=jnp.int32)[:, None]
    row_slot = row_kinds % 8
    in_layers = row_kinds < 8 * L
    normal_draw = jnp.clip(jax.random.normal(key, (row_total, D), jnp.float32), -4.0, 4.0)
    spread = jax.random.uniform(jax.random.fold_in(key, 7), (row_total, D), jnp.float32, -1.2, 0.4)
    position = jnp.arange(D, dtype=jnp.float32)[None, :] / D
    ramp = 0.5 + position
    gain_like = (1.0 + 0.15 * normal_draw) * ramp
    shift_like = 0.3 * normal_draw
    gamma_like = jnp.exp(spread) * ramp
    is_gain = in_layers & ((row_slot == 0) | (row_slot == 4)) | (row_kinds == 8 * L)
    is_gamma = in_layers & ((row_slot == 3) | (row_slot == 7))
    is_token = (row_kinds == 8 * L + 3) | (row_kinds == 8 * L + 4)
    return jnp.where(is_gain, gain_like, jnp.where(is_gamma, gamma_like, jnp.where(is_token, normal_draw, shift_like)))


def gradient_size():
    total = L * D * (3 + FF // D) * D + L * 5 * D * D + P_SIZE * D + D * V + L * 6 * D + (8 * L + 5) * D + H * NREL + V
    return 3.0 / total ** 0.5


def draw_states(key, shape):
    typical = gradient_size()
    first_moment = jnp.clip(jax.random.normal(jax.random.fold_in(key, 1), shape, jnp.float32), -4.0, 4.0) * (typical * 0.1 / 0.9)
    spread = jax.random.uniform(jax.random.fold_in(key, 2), shape, jnp.float32, -0.58, 0.58)
    second_root = typical * (0.001 / 0.999) ** 0.5 * jnp.exp(spread)
    return jnp.stack([first_moment, second_root])


def draw_in_moments(key, part):
    return draw_states(key, (L, D, 3 + FF // D, D))


def draw_out_moments(key, part):
    return draw_states(key, (L, 5, D, D))


def draw_patch_moments(key, part):
    return draw_states(key, (P_SIZE, D))


def draw_code_moments(key, part):
    return draw_states(key, (D, V))


def draw_bias_moments(key, part):
    return draw_states(key, (L, 6, D))


def draw_vector_moments(key, part):
    return draw_states(key, (8 * L + 5, D))


def draw_table_moments(key, part):
    return draw_states(key, (H, NREL))


def draw_logit_moments(key, part):
    return draw_states(key, (V,))


def plant(values, rng, low, largest):
    extent = values.shape
    place = [jax.random.randint(jax.random.fold_in(rng, axis), (), 0, extent[axis]) for axis in range(len(extent))]
    values = values.at[tuple(place)].set(low)
    longest = extent.index(max(extent))
    place[longest] = (place[longest] + 1) % extent[longest]
    return values.at[tuple(place)].set(largest)


def with_spikes(entries, rng, source, target, shards_of, factor):
    def block_of(dim):
        return (jnp.arange(entries.shape[dim]) // (entries.shape[dim] // shards_of)).reshape((-1,) + (1,) * (entries.ndim - 1 - dim))

    first = jax.random.permutation(rng, shards_of)[block_of(target)]
    second = (block_of(target) + shards_of // 2) % shards_of
    return jnp.where((block_of(source) == first) | (block_of(source) == second), factor * entries, entries)


def shard_levels(stream_key, dims, cuts, least, high):
    gain, own = 1.0, jax.random.fold_in(stream_key, 6)
    for dim, parts in cuts:
        heights = jnp.exp(jax.random.uniform(jax.random.fold_in(own, dim), (parts,), jnp.float32, least / len(cuts), high / len(cuts)))
        gain = gain * jnp.repeat(heights, dims[dim] // parts).reshape([-1 if axis == dim else 1 for axis in range(len(dims))])
    return gain


def noise(rng, shape, scale, most, shards=(), held_as=jnp.bfloat16):
    entries = jax.random.normal(rng, shape, jnp.float32) * scale
    if len(shards) > 0:
        entries = shard_levels(rng, shape, shards, -0.22, 0.18) * entries
    return jnp.clip(entries, min=-most, max=most).astype(held_as)


def gaussian_with(key, dims, deviation, most, cuts, heavy, kind=jnp.bfloat16):
    values = deviation * jax.random.normal(key, dims, jnp.float32)
    if cuts:
        values = values * shard_levels(key, dims, cuts, -0.22, 0.18)
    return jnp.clip(with_spikes(values, jax.random.fold_in(key, 3), *heavy), -most, most).astype(kind)


def setup_inputs(seed: int = 0) -> dict:
    seeds = jax.random.split(jax.random.key(seed), 22)
    images = gaussian_with(seeds[0], (IMAGES, NPATCH, P_SIZE), 1.0, 6.0, ((0, 8),), (0, 2, 8, 2.0))
    mask_places = draw_mask_places(jax.random.fold_in(seeds[21], 71), 0)
    mask_counts = draw_mask_counts(jax.random.fold_in(seeds[21], 71), 0)
    codes = plant(jax.random.randint(seeds[3], (IMAGES, NPATCH), 0, V), jax.random.fold_in(seeds[3], 1), 0, V - 1).astype(jnp.int32)
    step_count = jax.random.randint(seeds[4], (1,), 1, 21).astype(jnp.int32)
    in_weights = noise(seeds[5], (L, D, 3 + FF // D, D), D ** -0.5, 0.21875, ((1, 8), (3, 4)), jnp.float32)
    in_moments = draw_in_moments(jax.random.fold_in(seeds[21], 71), 0)
    out_weights = draw_out_weights(jax.random.fold_in(seeds[21], 71), 0)
    out_moments = draw_out_moments(jax.random.fold_in(seeds[21], 71), 0)
    patch_weight = noise(seeds[9], (P_SIZE, D), P_SIZE ** -0.5, 0.21875, ((0, 8),), jnp.float32)
    patch_moments = draw_patch_moments(jax.random.fold_in(seeds[21], 71), 0)
    code_weight = noise(seeds[11], (D, V), (D // 4) ** -0.5, 0.4375, ((0, 8), (1, 4)), jnp.float32)
    code_moments = draw_code_moments(jax.random.fold_in(seeds[21], 71), 0)
    in_biases = noise(seeds[13], (L, 6, D), 0.3, 4.0, ((2, 4),), jnp.float32)
    bias_moments = draw_bias_moments(jax.random.fold_in(seeds[21], 71), 0)
    vectors = draw_vectors(jax.random.fold_in(seeds[21], 71), 0)
    vector_moments = draw_vector_moments(jax.random.fold_in(seeds[21], 71), 0)
    rel_table = noise(seeds[17], (H, NREL), 0.5, 6.0, ((0, 4),), jnp.float32)
    table_moments = draw_table_moments(jax.random.fold_in(seeds[21], 71), 0)
    logit_bias = noise(seeds[19], (V,), 0.5, 6.0, ((0, 4),), jnp.float32)
    logit_moments = draw_logit_moments(jax.random.fold_in(seeds[21], 71), 0)
    return {"images": images, "mask_places": mask_places, "mask_counts": mask_counts, "codes": codes, "step_count": step_count, "in_weights": in_weights, "in_moments": in_moments, "out_weights": out_weights, "out_moments": out_moments, "patch_weight": patch_weight, "patch_moments": patch_moments, "code_weight": code_weight, "code_moments": code_moments, "in_biases": in_biases, "bias_moments": bias_moments, "vectors": vectors, "vector_moments": vector_moments, "rel_table": rel_table, "table_moments": table_moments, "logit_bias": logit_bias, "logit_moments": logit_moments}


EPS_NORM = 1e-06
CLIP_NORM = 3.0
LEARN_RATE = 0.1
BETA_ONE = 0.9
BETA_TWO = 0.999
ADAM_EPS = 1e-08
WEIGHT_DECAY = 0.05
HIGHEST = lax.Precision.HIGHEST

@jax.custom_vjp
def low(v):
    return lax.optimization_barrier(v.astype(jnp.bfloat16)).astype(jnp.float32)

@jax.custom_vjp
def low_back(v):
    return v

def low_keep(v):
    return (low(v), None)

def low_pass(kept, grad):
    return (grad,)

def back_keep(v):
    return (v, None)

def back_low(kept, grad):
    return (low(grad),)
low.defvjp(low_keep, low_pass)
low_back.defvjp(back_keep, back_low)

def rounded(value):
    return low(low_back(value))

def matmul(left_side, right_side):
    return jnp.matmul(left_side, right_side, precision=HIGHEST)

def layer_norm(row_block, gain_row, shift_row):
    average = lax.optimization_barrier(jnp.mean(row_block, axis=-1, keepdims=True))
    centred = row_block - average
    spread = lax.optimization_barrier(jnp.mean(centred * centred, axis=-1, keepdims=True))
    return centred * lax.rsqrt(spread + EPS_NORM) * gain_row + shift_row

def relative_index(grid_side, table_size):
    cells = jnp.arange(grid_side * grid_side, dtype=jnp.int32)
    row_of = cells // grid_side
    col_of = cells % grid_side
    inner_part = (row_of[:, None] - row_of[None, :] + grid_side - 1) * (2 * grid_side - 1) + (col_of[:, None] - col_of[None, :] + grid_side - 1)
    first_row = jnp.full((1, grid_side * grid_side), table_size - 3, jnp.int32)
    first_col = jnp.full((grid_side * grid_side, 1), table_size - 2, jnp.int32)
    corner = jnp.full((1, 1), table_size - 1, jnp.int32)
    upper = jnp.concatenate([corner, first_row], axis=1)
    lower = jnp.concatenate([first_col, inner_part.astype(jnp.int32)], axis=1)
    return jnp.concatenate([upper, lower], axis=0).astype(jnp.int32)

def block_loss(parameters, patches, places, counts, targets):
    in_weights, out_weights, patch_weight, code_weight, in_biases, vectors, rel_table, logit_bias = parameters
    images = patches.shape[0]
    part_width = D // N_TENSOR
    head_share = H // N_TENSOR
    code_share = V // N_TENSOR
    final_row = 8 * L
    slots = jnp.arange(MASK, dtype=jnp.int32)
    live_slots = (slots[None, :] < counts[:, None]).astype(jnp.float32)
    matches = (places[:, :, None] == jnp.arange(NPATCH, dtype=jnp.int32)[None, None, :]).astype(jnp.float32)
    covered = lax.optimization_barrier(jnp.sum(matches * live_slots[:, :, None], axis=1))[:, :, None]
    embedded = low_back(matmul(patches, low(patch_weight))) + vectors[final_row + 2]
    embedded = embedded * (1.0 - covered) + vectors[final_row + 4] * covered
    leading = jnp.broadcast_to(vectors[final_row + 3], (images, 1, D))
    stream = jnp.concatenate([leading, embedded], axis=1)
    table_bias = rel_table[:, relative_index(GRID, NREL)]
    for i in range(L):
        row_base = 8 * i
        normed = low(layer_norm(stream, vectors[row_base], vectors[row_base + 1]))
        branch = jnp.zeros((images, SEQ, D), jnp.float32)
        for g in range(N_TENSOR):
            columns = slice(g * part_width, (g + 1) * part_width)
            joined = in_weights[i, :, 0:3, columns].reshape(D, 3 * part_width)
            shifts = jnp.concatenate([in_biases[i, 0, columns], jnp.zeros((part_width,), jnp.float32), in_biases[i, 1, columns]])
            projected = rounded(matmul(low_back(normed), low(joined)) + shifts)
            queries = projected[..., :part_width].reshape(images, SEQ, head_share, HD)
            key_rows = projected[..., part_width:2 * part_width].reshape(images, SEQ, head_share, HD)
            value_rows = projected[..., 2 * part_width:].reshape(images, SEQ, head_share, HD)
            scores = jnp.einsum('bqhe,bkhe->bhqk', queries, key_rows, precision=HIGHEST) * 0.125
            scores = low_back(scores + table_bias[g * head_share:(g + 1) * head_share])
            softmax_rows = low(jax.nn.softmax(scores, axis=-1))
            attended = jnp.einsum('bhqk,bkhe->bqhe', softmax_rows, value_rows, precision=HIGHEST)
            attended = rounded(attended.reshape(images, SEQ, part_width))
            branch = branch + low(matmul(attended, low(out_weights[i, 0, columns, :])))
        middle = stream + vectors[row_base + 3] * (low_back(branch) + vectors[row_base + 2])
        normed = low(layer_norm(middle, vectors[row_base + 4], vectors[row_base + 5]))
        branch = jnp.zeros((images, SEQ, D), jnp.float32)
        for g in range(N_TENSOR):
            columns = slice(g * part_width, (g + 1) * part_width)
            upward = in_weights[i, :, 3:, columns].reshape(D, 4 * part_width)
            pre_act = low_back(matmul(low_back(normed), low(upward)) + in_biases[i, 2:, columns].reshape(4 * part_width))
            active = low(jax.nn.gelu(pre_act, approximate=False))
            downward = out_weights[i, 1:, columns, :].reshape(4 * part_width, D)
            branch = branch + low(matmul(active, low(downward)))
        stream = middle + vectors[row_base + 7] * (low_back(branch) + vectors[row_base + 6])
    closing = layer_norm(stream, vectors[final_row], vectors[final_row + 1])
    picked = low(jnp.take_along_axis(closing, (places + 1)[:, :, None], axis=1))
    wanted = jnp.take_along_axis(targets, places, axis=1)
    pieces = []
    for g in range(N_TENSOR):
        columns = slice(g * code_share, (g + 1) * code_share)
        pieces.append(low_back(matmul(low_back(picked), low(code_weight[:, columns])) + logit_bias[columns]))
    logits = jnp.concatenate(pieces, axis=-1)
    logsum = jax.nn.logsumexp(logits, axis=-1)
    chosen = jnp.take_along_axis(logits, wanted[:, :, None], axis=-1)[:, :, 0]
    return jnp.sum(live_slots * (logsum - chosen))

def adam_step(master, moments, gradient, clip_factor, step_number, decay_rate):
    clipped = gradient * clip_factor
    first_moment = BETA_ONE * moments[0] + (1.0 - BETA_ONE) * clipped
    second_root = jnp.sqrt(BETA_TWO * moments[1] * moments[1] + (1.0 - BETA_TWO) * clipped * clipped)
    first_fix = 1.0 - jnp.power(BETA_ONE, step_number)
    second_fix = 1.0 - jnp.power(BETA_TWO, step_number)
    direction = first_moment / first_fix / (second_root / jnp.sqrt(second_fix) + ADAM_EPS) + decay_rate * master
    return (master - LEARN_RATE * direction, jnp.stack([first_moment, second_root]))

def reference(images, mask_places, mask_counts, codes, step_count, in_weights, in_moments, out_weights, out_moments, patch_weight, patch_moments, code_weight, code_moments, in_biases, bias_moments, vectors, vector_moments, rel_table, table_moments, logit_bias, logit_moments):
    parameters = (in_weights, out_weights, patch_weight, code_weight, in_biases, vectors, rel_table, logit_bias)
    per_block = MB * IMG_MB
    block_count = IMAGES // per_block
    blocks_data = (images.astype(jnp.float32).reshape(block_count, per_block, NPATCH, P_SIZE), mask_places.reshape(block_count, per_block, MASK), mask_counts.reshape(block_count, per_block), codes.reshape(block_count, per_block, NPATCH))
    total_count = jnp.sum(mask_counts).astype(jnp.float32)
    checked = jax.checkpoint(block_loss)

    def whole_loss(weights):

        def advance(running, block_data):
            return (running + checked(weights, *block_data), None)
        summed, _ = lax.scan(advance, jnp.zeros((), jnp.float32), blocks_data)
        return summed / total_count
    loss_value, pullback = jax.vjp(whole_loss, parameters)
    gradients = pullback(jnp.ones((), jnp.float32))[0]
    squares = jnp.zeros((), jnp.float32)
    for gradient in gradients:
        squares = squares + jnp.sum(gradient * gradient)
    grad_norm = jnp.sqrt(squares)
    clip_factor = jnp.minimum(1.0, CLIP_NORM / (grad_norm + 1e-06))
    step_number = step_count[0].astype(jnp.float32)
    in_master, in_state = adam_step(in_weights, in_moments, gradients[0], clip_factor, step_number, WEIGHT_DECAY)
    out_master, out_state = adam_step(out_weights, out_moments, gradients[1], clip_factor, step_number, WEIGHT_DECAY)
    patch_master, patch_state = adam_step(patch_weight, patch_moments, gradients[2], clip_factor, step_number, WEIGHT_DECAY)
    code_master, code_state = adam_step(code_weight, code_moments, gradients[3], clip_factor, step_number, WEIGHT_DECAY)
    bias_master, bias_state = adam_step(in_biases, bias_moments, gradients[4], clip_factor, step_number, 0.0)
    vector_master, vector_state = adam_step(vectors, vector_moments, gradients[5], clip_factor, step_number, 0.0)
    table_master, table_state = adam_step(rel_table, table_moments, gradients[6], clip_factor, step_number, 0.0)
    logit_master, logit_state = adam_step(logit_bias, logit_moments, gradients[7], clip_factor, step_number, 0.0)
    return (loss_value.reshape(1), grad_norm.reshape(1), in_master, in_state, out_master, out_state, patch_master, patch_state, code_master, code_state, bias_master, bias_state, vector_master, vector_state, table_master, table_state, logit_master, logit_state)
```

```python
import functools

import jax
import jax.numpy as jnp
from jax import lax
from jax.experimental import pallas as pl
from jax.experimental.pallas import tpu as pltpu
from jax.sharding import PartitionSpec as P

HD = 64
GRID = 14
SPAN = 27
NPATCH = 196
ROWS = 208
NREL = 732
WIDE = 768

EPS_NORM = 1e-06
CLIP_NORM = 3.0
LEARN_RATE = 0.1
BETA_ONE = 0.9
BETA_TWO = 0.999
ADAM_EPS = 1e-08
WEIGHT_DECAY = 0.05
MASKED = -1e30

BF = jnp.bfloat16
F32 = jnp.float32
HIGHEST = lax.Precision.HIGHEST


S_DP, S_TP, S_CORE, S_X, S_Z, S_COUNT0, S_COUNT1, S_TOTAL = range(8)


def dot_nn(left, right, precision=None):
    return lax.dot_general(
        left, right, (((1,), (0,)), ((), ())), precision=precision, preferred_element_type=F32
    )


def dot_nt(left, right, precision=None):
    return lax.dot_general(
        left, right, (((1,), (1,)), ((), ())), precision=precision, preferred_element_type=F32
    )


def dot_tn(left, right, precision=None):
    return lax.dot_general(
        left, right, (((0,), (0,)), ((), ())), precision=precision, preferred_element_type=F32
    )


def norm_parts(rows):
    average = jnp.mean(rows, axis=-1, keepdims=True)
    centred = rows - average
    inverse = lax.rsqrt(jnp.mean(centred * centred, axis=-1, keepdims=True) + EPS_NORM)
    return centred * inverse, inverse


def norm_back(upstream, gain, unit, inverse):
    scaled = upstream * gain
    return inverse * (
        scaled
        - jnp.mean(scaled, axis=-1, keepdims=True)
        - unit * jnp.mean(scaled * unit, axis=-1, keepdims=True)
    )


def column_sum(rows):
    return jnp.sum(rows, axis=0, keepdims=True)


def call(kernel, name, outs, args, scratch=(), flops=0):
    moved = sum(a.size * a.dtype.itemsize for a in args) + sum(
        o.size * o.dtype.itemsize for o in outs
    )
    return pl.pallas_call(
        kernel,
        name=name,
        out_shape=tuple(outs),
        in_specs=[pl.BlockSpec(memory_space=pltpu.SMEM)]
        + [pl.BlockSpec(memory_space=pltpu.VMEM)] * (len(args) - 1),
        out_specs=tuple(pl.BlockSpec(memory_space=pltpu.VMEM) for _ in outs),
        scratch_shapes=list(scratch),
        compiler_params=pltpu.CompilerParams(vmem_limit_bytes=60 * 1024 * 1024),
        cost_estimate=pl.CostEstimate(flops=flops, bytes_accessed=moved, transcendentals=0),
    )(*args)


def sds(shape, dtype):
    return jax.ShapeDtypeStruct(shape, dtype)


def dp_permute(value, bits, count):
    return lax.ppermute(value, "dp", [(i, i ^ bits) for i in range(count)])


def tp_permute(value, bits):
    return lax.ppermute(value, "tensor", [(i, i ^ bits) for i in range(4)])


def gather_blocks(block):
    count = lax.axis_size("dp")
    if count != 8:
        whole = lax.all_gather(block, "dp", axis=1, tiled=True)
        return [whole]
    along_z = [dp_permute(block, bits, count) for bits in (2, 4, 6)]
    across = dp_permute(block, 1, count)
    rest = [dp_permute(part, 1, count) for part in along_z]
    return [block, across, along_z[0], rest[0], along_z[1], rest[1], along_z[2], rest[2]]


def weight_scratch(blocks):
    pages, rows, wide = blocks[0].shape
    return pltpu.VMEM((pages, len(blocks), rows, wide), blocks[0].dtype)


def assemble(sc, block_refs, scratch):
    count = len(block_refs)
    own = sc[S_DP]
    for k, ref in enumerate(block_refs):
        place = lax.bitwise_xor(own, k) if count > 1 else 0
        scratch[:, place] = ref[...]
    pages, _, rows, wide = scratch.shape
    return lambda page: scratch[page].reshape(count * rows, wide)


def emit(sc, page, value, outs, scratch):
    value = value.astype(BF)
    if len(outs) == 1:
        outs[0][page] = value
        return
    keep, give = outs
    wide = value.shape[1]
    scratch[...] = value.reshape(scratch.shape)
    x = sc[S_X]
    for z in range(4):
        keep[page, z] = scratch[2 * z + x]
        give[page, z] = scratch[2 * z + 1 - x]


def grad_outs(pages, rows, wide, count):
    if count != 8:
        return [sds((pages, rows, wide), BF)]
    return [sds((pages, 4, rows // 8, wide), BF)] * 2


def grad_scratch(rows, wide):
    return pltpu.VMEM((8, rows // 8, wide), BF)


def sum_x_kernel(sc, keep, got, own, one, two, three, total):
    total[...] = keep[...].astype(F32) + got[...].astype(F32)
    z = sc[S_Z]
    own[...] = total[:, z]
    one[...] = total[:, lax.bitwise_xor(z, 1)].astype(BF)
    two[...] = total[:, lax.bitwise_xor(z, 2)].astype(BF)
    three[...] = total[:, lax.bitwise_xor(z, 3)].astype(BF)


def sum_z_kernel(sc, own, one, two, three, total, squares):
    value = (own[...] + one[...].astype(F32)) + (two[...].astype(F32) + three[...].astype(F32))
    total[...] = value
    rows = jnp.sum(value * value, axis=0)
    squares[...] = jnp.broadcast_to(jnp.sum(rows), (8, 128))


def square_kernel(sc, value, squares):
    held = value[...]
    squares[...] = jnp.broadcast_to(jnp.sum(jnp.sum(held * held, axis=0)), (8, 128))


def scatter_sum(sc, grads):
    count = lax.axis_size("dp")
    if count != 8:
        shard = lax.psum_scatter(grads[0].astype(F32), "dp", scatter_dimension=1, tiled=True)
        (squares,) = call(square_kernel, "square", [sds((8, 128), F32)], (sc, shard))
        return shard, squares
    keep, give = grads
    got = dp_permute(give, 1, count)
    pages, _, rows, wide = keep.shape
    block = (pages, rows, wide)
    own, one, two, three = call(
        sum_x_kernel,
        "sum_x",
        [sds(block, F32)] + [sds(block, BF)] * 3,
        (sc, keep, got),
        [pltpu.VMEM(keep.shape, F32)],
    )
    one = dp_permute(one, 2, count)
    two = dp_permute(two, 4, count)
    three = dp_permute(three, 6, count)
    return call(
        sum_z_kernel,
        "sum_z",
        [sds(block, F32), sds((8, 128), F32)],
        (sc, own, one, two, three),
    )


def dp_sum(value):
    count = lax.axis_size("dp")
    if count != 8:
        return lax.psum(value, "dp")
    value = value + dp_permute(value, 1, count)
    one, two, three = (dp_permute(value, bits, count) for bits in (2, 4, 6))
    return (value + one) + (two + three)


def tensor_sum(keep, send):
    pair = (keep.astype(F32) + tp_permute(send, 1).astype(F32)).astype(BF)
    own = pair.astype(F32) + tp_permute(pair, 2).astype(F32)
    return own, tp_permute(own, 1)


def spread_matrix(dtype):
    j = lax.broadcasted_iota(jnp.int32, (ROWS, 384), 0)
    k = lax.broadcasted_iota(jnp.int32, (ROWS, 384), 1)
    tall = lax.shift_right_logical(j * 4682, 16)
    place = SPAN * (GRID - 1 - tall) + (GRID - 1) - (j - GRID * tall)
    return jnp.where((place == k) & (j < NPATCH), 1.0, 0.0).astype(dtype)


def table_kernel(sc, table, bias, stage):
    heads = table.shape[0]
    spread = spread_matrix(F32)
    row16 = lax.broadcasted_iota(jnp.int32, (16, WIDE), 0)
    i = lax.broadcasted_iota(jnp.int32, (ROWS, ROWS), 0)
    j = lax.broadcasted_iota(jnp.int32, (ROWS, ROWS), 1)
    for h in range(heads):
        line = jnp.concatenate([table[h : h + 1, :], jnp.zeros((1, WIDE - NREL), F32)], axis=1)
        wide = jnp.broadcast_to(line, (16, WIDE))
        shifted = wide
        for c in range(1, GRID):
            shifted = jnp.where(row16 == c, pltpu.roll(wide, WIDE - c, 1), shifted)
        stage[...] = jnp.zeros(stage.shape, F32)
        for r in range(GRID):
            turned = shifted if r == 0 else pltpu.roll(shifted, WIDE - SPAN * r, 1)
            stage[GRID * r : GRID * r + 16, :] = turned[:, 0:384]
        inner = dot_nt(stage[...], spread, HIGHEST)
        to_all = table[h : h + 1, NREL - 3 : NREL - 2]
        to_class = table[h : h + 1, NREL - 2 : NREL - 1]
        corner = table[h : h + 1, NREL - 1 : NREL]
        inner = jnp.where(i == NPATCH, jnp.where(j == NPATCH, corner, to_all), jnp.where(j == NPATCH, to_class, inner))
        inner = jnp.where(i > NPATCH, 0.0, inner)
        bias[h] = jnp.where(j > NPATCH, MASKED, inner)


def covered_rows(sc, places, image):
    slots = places.shape[1]
    patch = lax.broadcasted_iota(jnp.int32, (NPATCH, slots), 0)
    slot = lax.broadcasted_iota(jnp.int32, (NPATCH, slots), 1)
    hit = (patch == places[image : image + 1, :]) & (slot < sc[S_COUNT0 + image])
    return jnp.max(jnp.where(hit, 1.0, 0.0), axis=1, keepdims=True)


def picks(places, image, slots):
    row = lax.broadcasted_iota(jnp.int32, (slots, ROWS), 1)
    return row == places[image * slots : (image + 1) * slots, :]


def heads_of(array, image, h, first=0):
    return array[image * ROWS : (image + 1) * ROWS, first + HD * h : first + HD * (h + 1)]


def attend_kernel(blocks, sc, images, places, vectors, biases, bias, *refs):
    weight_refs = refs[:blocks]
    stream_ref, qk_ref, v_ref, heads_ref, keep, send, weights, term = refs[blocks:]
    share = v_ref.shape[1]
    page = assemble(sc, weight_refs, weights)
    final = vectors.shape[0] - 5
    left, right = page(2), page(3)
    for b in range(2):
        held = images[b]
        covered = covered_rows(sc, places, b)
        embedded = jnp.concatenate([dot_nn(held, left), dot_nn(held, right)], axis=1)
        embedded = embedded + vectors[final + 2 : final + 3, :]
        embedded = embedded * (1.0 - covered) + vectors[final + 4 : final + 5, :] * covered
        stream_ref[b, 192:ROWS, :] = jnp.zeros((ROWS - 192, WIDE), F32)
        stream_ref[b, 0:NPATCH, :] = embedded
        stream_ref[b, NPATCH : NPATCH + 1, :] = vectors[final + 3 : final + 4, :]
    unit, _ = norm_parts(stream_ref[...].reshape(2 * ROWS, WIDE))
    entered = (unit * vectors[0:1, :] + vectors[1:2, :]).astype(BF)
    joined = dot_nn(entered, page(0))
    shift = jnp.concatenate([biases[0, 0:1, :], jnp.zeros((1, share), F32)], axis=1)
    qk_ref[...] = (joined + shift).astype(BF)
    second = page(1)
    v_ref[...] = (dot_nn(entered, second[:, 0:share]) + biases[0, 1:2, :]).astype(BF)
    for b in range(2):
        for h in range(share // HD):
            scores = dot_nt(heads_of(qk_ref, b, h), heads_of(qk_ref, b, h, share)) * 0.125 + bias[h]
            scores = jnp.exp(scores - jnp.max(scores, axis=1, keepdims=True))
            soft = scores / jnp.sum(scores, axis=1, keepdims=True)
            heads_ref[b * ROWS : (b + 1) * ROWS, HD * h : HD * (h + 1)] = dot_nn(
                soft.astype(BF), heads_of(v_ref, b, h)
            ).astype(BF)
    term[...] = dot_nt(heads_ref[...], second[:, share:]).astype(BF).reshape(term.shape)
    keep[...] = term[sc[S_CORE]]
    send[...] = term[1 - sc[S_CORE]]


def add_branch(sc, out, base, own, other, gamma, shift):
    core = sc[S_CORE]
    out[core] = base[core] + gamma * (own[...] + shift)
    out[1 - core] = base[1 - core] + gamma * (other[...] + shift)


def feed_kernel(blocks, sc, stream, own, other, vectors, biases, *refs):
    weight_refs = refs[:blocks]
    middle, pre_ref, active_ref, keep, send, weights, term = refs[blocks:]
    page = assemble(sc, weight_refs, weights)
    add_branch(sc, middle, stream, own, other, vectors[3:4, :], vectors[2:3, :])
    unit, _ = norm_parts(middle[...].reshape(2 * ROWS, WIDE))
    entered = (unit * vectors[4:5, :] + vectors[5:6, :]).astype(BF)
    total = None
    half = WIDE // 2
    for g in range(2):
        shift = jnp.concatenate([biases[0, 2 + 2 * g : 3 + 2 * g, :], biases[0, 3 + 2 * g : 4 + 2 * g, :]], axis=1)
        pre = dot_nn(entered, page(g)) + shift
        pre_ref[:, half * g : half * (g + 1)] = pre
        active = (0.5 * pre * (1.0 + lax.erf(pre * 0.7071067811865476))).astype(BF)
        active_ref[:, half * g : half * (g + 1)] = active
        part = dot_nt(active, page(2 + g))
        total = part if total is None else total + part
    term[...] = total.astype(BF).reshape(term.shape)
    keep[...] = term[sc[S_CORE]]
    send[...] = term[1 - sc[S_CORE]]


def logit_kernel(blocks, sc, middle, own, other, vectors, places, codes, logit_bias, *refs):
    weight_refs = refs[:blocks]
    stream, picked_ref, logits_ref, stats, weights = refs[blocks:]
    page = assemble(sc, weight_refs, weights)
    final = vectors.shape[0] - 5
    slots = places.shape[0] // 2
    add_branch(sc, stream, middle, own, other, vectors[7:8, :], vectors[6:7, :])
    wanted = []
    for b in range(2):
        unit, _ = norm_parts(stream[b])
        closing = (unit * vectors[final : final + 1, :] + vectors[final + 1 : final + 2, :]).astype(BF)
        hit = picks(places, b, slots)
        picked_ref[b * slots : (b + 1) * slots, :] = dot_nn(jnp.where(hit, 1.0, 0.0).astype(BF), closing).astype(BF)
        found = jnp.where(hit[:, 0:NPATCH], codes[b : b + 1, :].astype(F32), 0.0)
        wanted.append(jnp.sum(found, axis=1, keepdims=True))
    wanted = jnp.concatenate(wanted, axis=0)
    logits = dot_nn(picked_ref[...], page(0)) + logit_bias[...]
    logits_ref[...] = logits
    share = logits.shape[1]
    first = (sc[S_TP] * share).astype(F32)
    column = lax.broadcasted_iota(jnp.int32, logits.shape, 1).astype(F32)
    peak = jnp.max(logits, axis=1, keepdims=True)
    summed = jnp.sum(jnp.exp(logits - peak), axis=1, keepdims=True)
    chosen = jnp.sum(jnp.where(column == wanted - first, logits, 0.0), axis=1, keepdims=True)
    lane = lax.broadcasted_iota(jnp.int32, stats.shape, 1)
    stats[...] = jnp.where(lane == 0, peak, jnp.where(lane == 1, summed, jnp.where(lane == 2, chosen, wanted)))


def join_stats(one, two):
    peak = jnp.maximum(one[:, 0:1], two[:, 0:1])
    summed = one[:, 1:2] * jnp.exp(one[:, 0:1] - peak) + two[:, 1:2] * jnp.exp(two[:, 0:1] - peak)
    return peak, summed, one[:, 2:3] + two[:, 2:3]


def stats_kernel(sc, one, two, out):
    peak, summed, chosen = join_stats(one[...], two[...])
    lane = lax.broadcasted_iota(jnp.int32, out.shape, 1)
    out[...] = jnp.where(lane == 0, peak, jnp.where(lane == 1, summed, jnp.where(lane == 2, chosen, one[:, 3:4])))


def loss_kernel(blocks, sc, one, two, logits_ref, *refs):
    weight_refs = refs[:blocks]
    grad_ref, shift_ref, loss_ref, keep, send, weights, term = refs[blocks:]
    page = assemble(sc, weight_refs, weights)
    logits = logits_ref[...]
    slots = logits.shape[0] // 2
    share = logits.shape[1]
    peak, summed, chosen = join_stats(one[...], two[...])
    logsum = peak + jnp.log(summed)
    slot = lax.broadcasted_iota(jnp.int32, (2 * slots, 1), 0)
    live = jnp.where(
        slot < slots,
        jnp.where(slot < sc[S_COUNT0], 1.0, 0.0),
        jnp.where(slot - slots < sc[S_COUNT1], 1.0, 0.0),
    )
    total = jnp.full((2 * slots, 1), sc[S_TOTAL], jnp.int32).astype(F32)
    loss_ref[...] = jnp.broadcast_to(column_sum(live * (logsum - chosen)), loss_ref.shape)
    first = (sc[S_TP] * share).astype(F32)
    column = lax.broadcasted_iota(jnp.int32, logits.shape, 1).astype(F32)
    matched = jnp.where(column == one[:, 3:4] - first, 1.0, 0.0)
    grad = ((live / total) * (jnp.exp(logits - logsum) - matched)).astype(BF)
    grad_ref[...] = grad
    shift_ref[...] = column_sum(grad.astype(F32))
    term[...] = dot_nt(grad, page(0)).astype(BF).reshape(term.shape)
    keep[...] = term[sc[S_CORE]]
    send[...] = term[1 - sc[S_CORE]]


def code_grad_kernel(sc, picked, grad, *refs):
    outs, scratch = refs[:-1], refs[-1]
    emit(sc, 0, dot_tn(picked[...], grad[...]), outs, scratch)


def branch_back(sc, gated_ref, sums, first, upstream, own, other, gamma, shift):
    core = sc[S_CORE]
    gamma_sum = column_sum(upstream[core] * (own[...] + shift)) + column_sum(
        upstream[1 - core] * (other[...] + shift)
    )
    sums[first + 1 : first + 2, :] = gamma_sum
    gated = upstream[...].reshape(2 * ROWS, WIDE) * gamma
    sums[first : first + 1, :] = column_sum(gated)
    gated_ref[...] = gated.astype(BF)


def feed_back_kernel(blocks, sc, own, other, places, stream, branch_own, branch_other, vectors, pre_ref, *refs):
    weight_refs = refs[:blocks]
    upstream, gated_ref, grad_pre_ref, sums, keep, send, weights, term, picked = refs[blocks:]
    page = assemble(sc, weight_refs, weights)
    core = sc[S_CORE]
    final = vectors.shape[0] - 5
    slots = places.shape[0] // 2
    picked[core] = own[...]
    picked[1 - core] = other[...]
    gain_sum = jnp.zeros((1, WIDE), F32)
    shift_sum = jnp.zeros((1, WIDE), F32)
    for b in range(2):
        hit = jnp.where(picks(places, b, slots), 1.0, 0.0).astype(F32)
        closing = dot_tn(hit, picked[b], HIGHEST)
        unit, inverse = norm_parts(stream[b])
        gain_sum += column_sum(closing * unit)
        shift_sum += column_sum(closing)
        upstream[b] = norm_back(closing, vectors[final : final + 1, :], unit, inverse)
    sums[0:1, :] = gain_sum
    sums[1:2, :] = shift_sum
    branch_back(sc, gated_ref, sums, 2, upstream, branch_own, branch_other, vectors[7:8, :], vectors[6:7, :])
    gated = gated_ref[...]
    total = None
    half = WIDE // 2
    for g in range(2):
        pre = pre_ref[:, half * g : half * (g + 1)]
        grad_active = dot_nn(gated, page(2 + g))
        slope = 0.5 * (1.0 + lax.erf(pre * 0.7071067811865476)) + pre * (
            jnp.exp(-0.5 * pre * pre) * 0.3989422804014327
        )
        grad_pre = (grad_active * slope).astype(BF)
        grad_pre_ref[:, half * g : half * (g + 1)] = grad_pre
        sums[4:5, half * g : half * (g + 1)] = column_sum(grad_pre.astype(F32))
        part = dot_nt(grad_pre, page(g))
        total = part if total is None else total + part
    term[...] = total.astype(BF).reshape(term.shape)
    keep[...] = term[core]
    send[...] = term[1 - core]


def up_grad_kernel(sc, middle, vectors, grad_pre, *refs):
    outs, scratch = refs[:-1], refs[-1]
    half = WIDE // 2
    unit, _ = norm_parts(middle[...].reshape(2 * ROWS, WIDE))
    entered = (unit * vectors[4:5, :] + vectors[5:6, :]).astype(BF)
    for g in range(2):
        emit(sc, g, dot_tn(entered, grad_pre[:, half * g : half * (g + 1)]), outs, scratch)


def down_grad_kernel(sc, gated, active, *refs):
    outs, scratch = refs[:-1], refs[-1]
    half = WIDE // 2
    for g in range(2):
        emit(sc, g, dot_tn(gated[...], active[:, half * g : half * (g + 1)]), outs, scratch)


def attend_back_kernel(
    blocks, sc, own, other, upstream, middle, branch_own, branch_other, vectors, qk, v, bias, *refs
):
    weight_refs = refs[:blocks]
    passed, gated_ref, grad_qk, grad_v, sums, table_sums, keep, send, weights, term, grad_heads, stage = refs[blocks:]
    page = assemble(sc, weight_refs, weights)
    core = sc[S_CORE]
    share = v.shape[1]
    gain = vectors[4:5, :]
    gain_sum = jnp.zeros((1, WIDE), F32)
    shift_sum = jnp.zeros((1, WIDE), F32)
    for image, arrived in ((core, own), (1 - core, other)):
        grad = arrived[...]
        unit, inverse = norm_parts(middle[image])
        gain_sum += column_sum(grad * unit)
        shift_sum += column_sum(grad)
        passed[image] = upstream[image] + norm_back(grad, gain, unit, inverse)
    sums[0:1, :] = gain_sum
    sums[1:2, :] = shift_sum
    branch_back(sc, gated_ref, sums, 2, passed, branch_own, branch_other, vectors[3:4, :], vectors[2:3, :])
    second = page(1)
    grad_heads[...] = dot_nn(gated_ref[...], second[:, share:]).astype(BF)
    spread = spread_matrix(BF)
    lane = lax.broadcasted_iota(jnp.int32, (1, WIDE), 1)
    row16 = lax.broadcasted_iota(jnp.int32, (16, WIDE), 0)
    i = lax.broadcasted_iota(jnp.int32, (ROWS, ROWS), 0)
    j = lax.broadcasted_iota(jnp.int32, (ROWS, ROWS), 1)
    for h in range(share // HD):
        together = None
        spread_sum = None
        for b in range(2):
            rows = slice(b * ROWS, (b + 1) * ROWS)
            queries, keys, values = heads_of(qk, b, h), heads_of(qk, b, h, share), heads_of(v, b, h)
            scores = dot_nt(queries, keys) * 0.125 + bias[h]
            scores = jnp.exp(scores - jnp.max(scores, axis=1, keepdims=True))
            soft = scores / jnp.sum(scores, axis=1, keepdims=True)
            grad_out = heads_of(grad_heads, b, h)
            grad_v[rows, HD * h : HD * (h + 1)] = dot_tn(soft.astype(BF), grad_out).astype(BF)
            grad_soft = dot_nt(grad_out, values)
            grad_scores = soft * (grad_soft - jnp.sum(soft * grad_soft, axis=1, keepdims=True))
            grad_scores = grad_scores.astype(BF)
            grad_qk[rows, HD * h : HD * (h + 1)] = (dot_nn(grad_scores, keys) * 0.125).astype(BF)
            grad_qk[rows, share + HD * h : share + HD * (h + 1)] = (dot_tn(grad_scores, queries) * 0.125).astype(BF)
            wide = grad_scores.astype(F32)
            together = wide if together is None else together + wide
            part = dot_nn(grad_scores, spread)
            spread_sum = part if spread_sum is None else spread_sum + part
        stage[...] = spread_sum
        lined = jnp.zeros((16, WIDE), F32)
        for r in range(GRID):
            piece = jnp.concatenate([stage[GRID * r : GRID * r + 16, :], jnp.zeros((16, WIDE - 384), F32)], axis=1)
            lined += piece if r == 0 else pltpu.roll(piece, SPAN * r, 1)
        folded = jnp.where(row16 == 0, lined, 0.0)
        for c in range(1, GRID):
            folded += pltpu.roll(jnp.where(row16 == c, lined, 0.0), c, 1)
        line = column_sum(folded)
        on_row, on_column = i == NPATCH, j == NPATCH
        to_all = jnp.sum(jnp.where(on_row & (j < NPATCH), together, 0.0))
        to_class = jnp.sum(jnp.where(on_column & (i < NPATCH), together, 0.0))
        corner = jnp.sum(jnp.where(on_row & on_column, together, 0.0))
        line = jnp.where(lane == NREL - 3, to_all, line)
        line = jnp.where(lane == NREL - 2, to_class, line)
        line = jnp.where(lane == NREL - 1, corner, line)
        table_sums[h : h + 1, :] = line
    sums[4:5, 0:share] = column_sum(grad_qk[:, 0:share].astype(F32))
    sums[4:5, share : 2 * share] = column_sum(grad_v[...].astype(F32))
    sums[4:5, 2 * share :] = jnp.zeros((1, WIDE - 2 * share), F32)
    total = dot_nt(grad_qk[...], page(0)) + dot_nt(grad_v[...], second[:, 0:share])
    term[...] = total.astype(BF).reshape(term.shape)
    keep[...] = term[core]
    send[...] = term[1 - core]


def attend_grad_kernel(sc, stream, vectors, grad_qk, grad_v, gated, heads, *refs):
    outs, scratch = refs[:-1], refs[-1]
    unit, _ = norm_parts(stream[...].reshape(2 * ROWS, WIDE))
    entered = (unit * vectors[0:1, :] + vectors[1:2, :]).astype(BF)
    emit(sc, 0, dot_tn(entered, grad_qk[...]), outs, scratch)
    pair = jnp.concatenate([dot_tn(entered, grad_v[...]), dot_tn(gated[...], heads[...])], axis=1)
    emit(sc, 1, pair, outs, scratch)


def embed_back_kernel(sc, own, other, passed, stream, vectors, images, places, feed_sums, attend_sums, table_sums, logit_sums, loss, *refs):
    small, outs = refs[0], refs[1:-2]
    scratch, grads = refs[-2], refs[-1]
    core = sc[S_CORE]
    share = attend_sums.shape[1] // 4
    gain = vectors[0:1, :]
    zero = jnp.zeros((1, WIDE), F32)
    gain_sum, shift_sum = zero, zero
    for image, arrived in ((core, own), (1 - core, other)):
        grad = arrived[...]
        unit, inverse = norm_parts(stream[image])
        gain_sum += column_sum(grad * unit)
        shift_sum += column_sum(grad)
        grads[image] = passed[image] + norm_back(grad, gain, unit, inverse)
    patch_sum, class_sum, mask_sum = zero, zero, zero
    halves = [None, None]
    for b in range(2):
        grad = grads[b, 0:NPATCH, :]
        covered = covered_rows(sc, places, b)
        through = grad * (1.0 - covered)
        patch_sum += column_sum(through)
        mask_sum += column_sum(grad * covered)
        class_sum += grads[b, NPATCH : NPATCH + 1, :]
        through = through.astype(BF)
        for g in range(2):
            part = dot_tn(images[b], through[:, g * 384 : (g + 1) * 384])
            halves[g] = part if halves[g] is None else halves[g] + part
    for g in range(2):
        emit(sc, g, halves[g], outs, scratch)
    small[...] = jnp.zeros(small.shape, F32)
    small[0:1, :] = gain_sum
    small[1:2, :] = shift_sum
    small[2:4, :] = attend_sums[2:4, :]
    small[4:6, :] = attend_sums[0:2, :]
    small[6:8, :] = feed_sums[2:4, :]
    small[8:10, :] = feed_sums[0:2, :]
    small[10:11, :] = patch_sum
    small[11:12, :] = class_sum
    small[12:13, :] = mask_sum
    small[13:14, :] = attend_sums[4:5, :]
    small[14:15, :] = feed_sums[4:5, :]
    heads = table_sums.shape[0]
    small[15 : 15 + heads, :] = table_sums[...]
    first = 15 + heads
    left = logit_sums.shape[1]
    row = 0
    while left > 0:
        take = min(left, WIDE)
        small[first + row : first + row + 1, 0:take] = logit_sums[:, row * WIDE : row * WIDE + take]
        left -= take
        row += 1
    small[first + row : first + row + 1, 0:128] = loss[...]


def small_square_kernel(dp, tp, heads, sc, small, squares):
    held = small[...]
    row = lax.broadcasted_iota(jnp.int32, held.shape, 0)
    weight = jnp.where(row < 13, 1.0 / (dp * tp), 1.0 / dp)
    weight = jnp.where(row < small.shape[0] - 1, weight, 0.0)
    squares[...] = jnp.broadcast_to(jnp.sum(jnp.sum(held * held * weight, axis=0)), (8, 128))


def adam(master, first_old, root_old, gradient, fix, decay):
    clip, first_fix, second_fix = fix
    clipped = gradient * clip
    first = BETA_ONE * first_old + (1.0 - BETA_ONE) * clipped
    root = jnp.sqrt(BETA_TWO * root_old * root_old + (1.0 - BETA_TWO) * clipped * clipped)
    direction = first / first_fix / (root / second_fix + ADAM_EPS) + decay * master
    return master - LEARN_RATE * direction, first, root


def adam_matrix_kernel(
    fix_ref, in_w, in_m, out_w, out_m, patch_w, patch_m, first, up, down, patch,
    in_master, in_state, out_master, out_state, patch_master, patch_state,
):
    fix = (fix_ref[0], fix_ref[1], fix_ref[2])
    share = in_w.shape[3]
    half = 2 * share

    def into(j, gradient):
        master, moment, root = adam(
            in_w[0, :, j, :], in_m[0, 0, :, j, :], in_m[1, 0, :, j, :], gradient, fix, WEIGHT_DECAY
        )
        in_master[0, :, j, :] = master
        in_state[0, 0, :, j, :] = moment
        in_state[1, 0, :, j, :] = root

    def outof(j, gradient):
        master, moment, root = adam(
            out_w[0, j], out_m[0, 0, j], out_m[1, 0, j], gradient.T, fix, WEIGHT_DECAY
        )
        out_master[0, j] = master
        out_state[0, 0, j] = moment
        out_state[1, 0, j] = root

    into(0, first[0, :, 0:share])
    into(1, first[0, :, share:half])
    into(2, first[1, :, 0:share])
    outof(0, first[1, :, share:half])
    for g in range(2):
        for k in range(2):
            into(3 + 2 * g + k, up[g, :, share * k : share * (k + 1)])
            outof(1 + 2 * g + k, down[g, :, share * k : share * (k + 1)])
    for g in range(2):
        columns = slice(g * half, (g + 1) * half)
        master, moment, root = adam(
            patch_w[:, columns], patch_m[0, :, columns], patch_m[1, :, columns], patch[g], fix, WEIGHT_DECAY
        )
        patch_master[:, columns] = master
        patch_state[0, :, columns] = moment
        patch_state[1, :, columns] = root


def adam_code_kernel(pieces, fix_ref, code_w, code_m, *refs):
    fix = (fix_ref[0], fix_ref[1], fix_ref[2])
    grads = refs[:pieces]
    code_master, code_state = refs[pieces:]
    wide = code_w.shape[1] // pieces
    for g in range(pieces):
        columns = slice(g * wide, (g + 1) * wide)
        master, moment, root = adam(
            code_w[:, columns], code_m[0, :, columns], code_m[1, :, columns], grads[g][0], fix, WEIGHT_DECAY
        )
        code_master[:, columns] = master
        code_state[0, :, columns] = moment
        code_state[1, :, columns] = root


def adam_small_kernel(
    fix_ref, small, bias_w, bias_m, vec_w, vec_m, table_w, table_m, logit_w, logit_m,
    bias_master, bias_state, vec_master, vec_state, table_master, table_state, logit_master, logit_state,
):
    fix = (fix_ref[0], fix_ref[1], fix_ref[2])
    share = bias_w.shape[2]
    for j in range(6):
        row, k = (13, j) if j < 2 else (14, j - 2)
        gradient = small[row : row + 1, share * k : share * (k + 1)]
        master, moment, root = adam(
            bias_w[0, j : j + 1, :], bias_m[0, 0, j : j + 1, :], bias_m[1, 0, j : j + 1, :], gradient, fix, 0.0
        )
        bias_master[0, j : j + 1, :] = master
        bias_state[0, 0, j : j + 1, :] = moment
        bias_state[1, 0, j : j + 1, :] = root
    vec_master[...], vec_state[0], vec_state[1] = adam(vec_w[...], vec_m[0], vec_m[1], small[0:13, :], fix, 0.0)
    heads = table_w.shape[0]
    table_master[...], table_state[0], table_state[1] = adam(
        table_w[...], table_m[0], table_m[1], small[15 : 15 + heads, 0:NREL], fix, 0.0
    )
    first = 15 + heads
    share = logit_w.shape[1]
    gradient = jnp.concatenate(
        [small[first + k : first + k + 1, 0 : min(WIDE, share - k * WIDE)] for k in range(-(-share // WIDE))], axis=1
    )
    master, moment, root = adam(logit_w[...], logit_m[0:1, :], logit_m[1:2, :], gradient, fix, 0.0)
    logit_master[...] = master
    logit_state[0:1, :] = moment
    logit_state[1:2, :] = root


def local(
    images, mask_places, mask_counts, codes, step_count,
    in_weights, in_moments, out_weights, out_moments, patch_weight, patch_moments,
    code_weight, code_moments, in_biases, bias_moments, vectors, vector_moments,
    rel_table, table_moments, logit_bias, logit_moments,
):
    dp = lax.axis_size("dp")
    tp = lax.axis_size("tensor")
    dp_index = lax.axis_index("dp").astype(jnp.int32)
    tp_index = lax.axis_index("tensor").astype(jnp.int32)
    share = in_weights.shape[3]
    code_share = code_weight.shape[1]
    slots = mask_places.shape[1]
    heads = rel_table.shape[0]
    own_counts = lax.dynamic_slice_in_dim(mask_counts, dp_index * 2, 2)
    total_count = jnp.sum(mask_counts)
    sc = jnp.stack(
        [dp_index, tp_index, tp_index & 1, dp_index & 1, dp_index >> 1, own_counts[0], own_counts[1], total_count]
    )

    into = in_weights[0].astype(BF)
    outof = out_weights[0].astype(BF).transpose(0, 2, 1)
    patch = patch_weight.astype(BF)

    def pair(one, two):
        return jnp.concatenate([one, two], axis=-1)

    first_group = jnp.stack(
        [pair(into[:, 0], into[:, 1]), pair(into[:, 2], outof[0]), patch[:, :384], patch[:, 384:]]
    )
    second_group = jnp.stack(
        [pair(into[:, 3], into[:, 4]), pair(into[:, 5], into[:, 6]), pair(outof[1], outof[2]), pair(outof[3], outof[4])]
    )
    code_group = code_weight.astype(BF)[None]
    first_blocks = gather_blocks(first_group)
    second_blocks = gather_blocks(second_group)
    code_blocks = gather_blocks(code_group)
    nb = len(first_blocks)

    (bias,) = call(
        table_kernel, "table", [sds((heads, ROWS, ROWS), F32)], (sc, rel_table), [pltpu.VMEM((ROWS, 384), F32)]
    )
    stacked = sds((2, ROWS, WIDE), F32)
    term_outs = [sds((ROWS, WIDE), BF)] * 2
    term_scratch = pltpu.VMEM((2, ROWS, WIDE), BF)
    places_column = mask_places.reshape(2 * slots, 1)
    matmul_flops = 2 * 2 * ROWS * WIDE

    stream, qk, v, attended, keep, send = call(
        functools.partial(attend_kernel, nb),
        "attend",
        [stacked, sds((2 * ROWS, 2 * share), BF), sds((2 * ROWS, share), BF), sds((2 * ROWS, share), BF)] + term_outs,
        (sc, images, mask_places, vectors, in_biases, bias, *first_blocks),
        [weight_scratch(first_blocks), term_scratch],
        matmul_flops * 2 * WIDE,
    )
    attend_own, attend_other = tensor_sum(keep, send)
    middle, pre, active, keep, send = call(
        functools.partial(feed_kernel, nb),
        "feed",
        [stacked, sds((2 * ROWS, WIDE), F32), sds((2 * ROWS, WIDE), BF)] + term_outs,
        (sc, stream, attend_own, attend_other, vectors, in_biases, *second_blocks),
        [weight_scratch(second_blocks), term_scratch],
        matmul_flops * 2 * WIDE,
    )
    feed_own, feed_other = tensor_sum(keep, send)
    last, picked, logits, stats = call(
        functools.partial(logit_kernel, nb),
        "logit",
        [stacked, sds((2 * slots, WIDE), BF), sds((2 * slots, code_share), F32), sds((2 * slots, 128), F32)],
        (sc, middle, feed_own, feed_other, vectors, places_column, codes, logit_bias.reshape(1, -1), *code_blocks),
        [weight_scratch(code_blocks)],
        matmul_flops * 2 * WIDE,
    )
    (stats,) = call(stats_kernel, "stats", [sds(stats.shape, F32)], (sc, stats, tp_permute(stats, 1)))
    other_stats = tp_permute(stats, 2)
    slot_outs = [sds((slots, WIDE), BF)] * 2
    grad_logits, logit_sums, loss, keep, send = call(
        functools.partial(loss_kernel, nb),
        "loss",
        [sds((2 * slots, code_share), BF), sds((1, code_share), F32), sds((1, 128), F32)] + slot_outs,
        (sc, stats, other_stats, logits, *code_blocks),
        [weight_scratch(code_blocks), pltpu.VMEM((2, slots, WIDE), BF)],
        matmul_flops * 2 * WIDE,
    )
    picked_own, picked_other = tensor_sum(keep, send)
    pieces = 4
    wide = code_share // pieces
    code_shards = []
    for g in range(pieces):
        grads = call(
            code_grad_kernel,
            "code_grad",
            grad_outs(1, WIDE, wide, dp),
            (sc, picked, grad_logits[:, g * wide : (g + 1) * wide]),
            [grad_scratch(WIDE, wide)],
            2 * 2 * slots * WIDE * wide,
        )
        code_shards.append(scatter_sum(sc, grads))

    upstream, gated, grad_pre, feed_sums, keep, send = call(
        functools.partial(feed_back_kernel, nb),
        "feed_back",
        [stacked, sds((2 * ROWS, WIDE), BF), sds((2 * ROWS, WIDE), BF), sds((8, WIDE), F32)] + term_outs,
        (sc, picked_own, picked_other, places_column, last, feed_own, feed_other, vectors, pre, *second_blocks),
        [weight_scratch(second_blocks), term_scratch, pltpu.VMEM((2, slots, WIDE), F32)],
        matmul_flops * 2 * WIDE,
    )
    feed_in_own, feed_in_other = tensor_sum(keep, send)
    pair_scratch = [grad_scratch(WIDE, 2 * share)]
    up_shard = scatter_sum(
        sc,
        call(
            up_grad_kernel, "up_grad", grad_outs(2, WIDE, 2 * share, dp), (sc, middle, vectors, grad_pre),
            pair_scratch, matmul_flops * WIDE,
        ),
    )
    down_shard = scatter_sum(
        sc,
        call(
            down_grad_kernel, "down_grad", grad_outs(2, WIDE, 2 * share, dp), (sc, gated, active),
            pair_scratch, matmul_flops * WIDE,
        ),
    )
    passed, gated, grad_qk, grad_v, attend_sums, table_sums, keep, send = call(
        functools.partial(attend_back_kernel, nb),
        "attend_back",
        [
            stacked, sds((2 * ROWS, WIDE), BF), sds((2 * ROWS, 2 * share), BF), sds((2 * ROWS, share), BF),
            sds((8, WIDE), F32), sds((heads, WIDE), F32),
        ]
        + term_outs,
        (sc, feed_in_own, feed_in_other, upstream, middle, attend_own, attend_other, vectors, qk, v, bias, *first_blocks),
        [weight_scratch(first_blocks), term_scratch, pltpu.VMEM((2 * ROWS, share), BF), pltpu.VMEM((ROWS, 384), F32)],
        matmul_flops * 2 * WIDE,
    )
    attend_in_own, attend_in_other = tensor_sum(keep, send)
    first_shard = scatter_sum(
        sc,
        call(
            attend_grad_kernel, "attend_grad", grad_outs(2, WIDE, 2 * share, dp),
            (sc, stream, vectors, grad_qk, grad_v, gated, attended), pair_scratch, matmul_flops * WIDE,
        ),
    )
    small_rows = 15 + heads + -(-code_share // WIDE) + 1
    embed_outs = call(
        embed_back_kernel,
        "embed_back",
        [sds((small_rows, WIDE), F32)] + grad_outs(2, WIDE, 384, dp),
        (
            sc, attend_in_own, attend_in_other, passed, stream, vectors, images, mask_places,
            feed_sums, attend_sums, table_sums, logit_sums, loss,
        ),
        [grad_scratch(WIDE, 384), pltpu.VMEM((2, ROWS, WIDE), F32)],
        matmul_flops * WIDE,
    )
    patch_shard = scatter_sum(sc, embed_outs[1:])
    small = dp_sum(embed_outs[0])
    (small_squares,) = call(
        functools.partial(small_square_kernel, dp, tp, heads), "small_square", [sds((8, 128), F32)], (sc, small)
    )
    squares = first_shard[1] + up_shard[1] + down_shard[1] + patch_shard[1] / tp + small_squares
    for shard in code_shards:
        squares = squares + shard[1]
    spread = lax.all_to_all(
        jnp.broadcast_to(squares[None], (dp * tp, 8, 128)), ("dp", "tensor"), 0, 0
    )
    total_squares = jnp.sum(spread[:, 0, 0])
    grad_norm = jnp.sqrt(total_squares)
    clip = jnp.minimum(1.0, CLIP_NORM / (grad_norm + 1e-06))
    step_number = step_count[0].astype(F32)
    fix = jnp.stack(
        [clip, 1.0 - jnp.power(BETA_ONE, step_number), jnp.sqrt(1.0 - jnp.power(BETA_TWO, step_number))]
    )
    loss_value = small[small_rows - 1, 0] / total_count.astype(F32)

    def like(array):
        return sds(array.shape, F32)

    in_master, in_state, out_master, out_state, patch_master, patch_state = call(
        adam_matrix_kernel,
        "adam_matrix",
        [like(a) for a in (in_weights, in_moments, out_weights, out_moments, patch_weight, patch_moments)],
        (
            fix, in_weights, in_moments, out_weights, out_moments, patch_weight, patch_moments,
            first_shard[0], up_shard[0], down_shard[0], patch_shard[0],
        ),
    )
    code_master, code_state = call(
        functools.partial(adam_code_kernel, pieces),
        "adam_code",
        [like(code_weight), like(code_moments)],
        (fix, code_weight, code_moments, *[shard[0] for shard in code_shards]),
    )
    logit_row = logit_bias.reshape(1, -1)
    bias_master, bias_state, vec_master, vec_state, table_master, table_state, logit_master, logit_state = call(
        adam_small_kernel,
        "adam_small",
        [
            like(a)
            for a in (
                in_biases, bias_moments, vectors, vector_moments, rel_table, table_moments, logit_row, logit_moments,
            )
        ],
        (
            fix, small, in_biases, bias_moments, vectors, vector_moments, rel_table, table_moments,
            logit_row, logit_moments,
        ),
    )
    return (
        loss_value.reshape(1), grad_norm.reshape(1),
        in_master, in_state, out_master, out_state, patch_master, patch_state,
        code_master, code_state, bias_master, bias_state, vec_master, vec_state,
        table_master, table_state, logit_master.reshape(-1), logit_state,
    )


def solution(mesh):
    in_specs = (
        P("dp", None, None),
        P("dp", None),
        P(),
        P("dp", None),
        P(),
        P(None, "dp", None, "tensor"),
        P(None, None, "dp", None, "tensor"),
        P(None, None, "tensor", "dp"),
        P(None, None, None, "tensor", "dp"),
        P("dp", None),
        P(None, "dp", None),
        P("dp", "tensor"),
        P(None, "dp", "tensor"),
        P(None, None, "tensor"),
        P(None, None, None, "tensor"),
        P(),
        P(),
        P("tensor", None),
        P(None, "tensor", None),
        P("tensor"),
        P(None, "tensor"),
    )
    out_specs = (P(), P()) + in_specs[5:]
    return jax.shard_map(local, mesh=mesh, in_specs=in_specs, out_specs=out_specs, check_vma=False)
```

```python
import functools

import jax
import jax.numpy as jnp
from jax import lax
from jax.experimental import pallas as pl
from jax.experimental.pallas import tpu as pltpu
from jax.sharding import PartitionSpec as P


HD = 64
GRID = 14
SPAN = 27
NPATCH = 196
ROWS = 208
NREL = 732
WIDE = 768

EPS_NORM = 1e-06
CLIP_NORM = 3.0
LEARN_RATE = 0.1
BETA_ONE = 0.9
BETA_TWO = 0.999
ADAM_EPS = 1e-08
WEIGHT_DECAY = 0.05
MASKED = -1e30

BF = jnp.bfloat16
F32 = jnp.float32


CODE_GROUPS = (10, 6)
CODE_PIECES = (5, 11)


S_DP, S_TP, S_CORE, S_X, S_Z, S_COUNT0, S_COUNT1, S_TOTAL = range(8)


def dot_nn(left, right):
    return lax.dot_general(left, right, (((1,), (0,)), ((), ())), preferred_element_type=F32)


def dot_nt(left, right):
    return lax.dot_general(left, right, (((1,), (1,)), ((), ())), preferred_element_type=F32)


def dot_tn(left, right):
    return lax.dot_general(left, right, (((0,), (0,)), ((), ())), preferred_element_type=F32)


def norm_parts(rows):
    average = jnp.mean(rows, axis=-1, keepdims=True)
    centred = rows - average
    inverse = lax.rsqrt(jnp.mean(centred * centred, axis=-1, keepdims=True) + EPS_NORM)
    return centred * inverse, inverse


def norm_back(upstream, gain, unit, inverse):
    scaled = upstream * gain
    return inverse * (
        scaled
        - jnp.mean(scaled, axis=-1, keepdims=True)
        - unit * jnp.mean(scaled * unit, axis=-1, keepdims=True)
    )


def column_sum(rows):
    return jnp.sum(rows, axis=0, keepdims=True)


def call(kernel, outs, args, scratch=(), flops=0, scalars=1, scalar_outs=0):
    moved = sum(a.size * a.dtype.itemsize for a in args) + sum(
        o.size * o.dtype.itemsize for o in outs
    )
    return pl.pallas_call(
        kernel,
        out_shape=tuple(outs),
        in_specs=[pl.BlockSpec(memory_space=pltpu.SMEM)] * scalars
        + [pl.BlockSpec(memory_space=pltpu.VMEM)] * (len(args) - scalars),
        out_specs=(pl.BlockSpec(memory_space=pltpu.VMEM),) * (len(outs) - scalar_outs)
        + (pl.BlockSpec(memory_space=pltpu.SMEM),) * scalar_outs,
        scratch_shapes=list(scratch),
        compiler_params=pltpu.CompilerParams(vmem_limit_bytes=60 * 1024 * 1024),
        cost_estimate=pl.CostEstimate(flops=flops, bytes_accessed=moved, transcendentals=0),
    )(*args)


def sds(shape, dtype):
    return jax.ShapeDtypeStruct(shape, dtype)


def dp_permute(value, bits, count):
    return lax.ppermute(value, "dp", [(i, i ^ bits) for i in range(count)])


def tp_permute(value, bits):
    return lax.ppermute(value, "tensor", [(i, i ^ bits) for i in range(4)])


def gather_blocks(block):
    count = lax.axis_size("dp")
    if count != 8:
        whole = lax.all_gather(block, "dp", axis=1, tiled=True)
        return [whole]
    along_z = [dp_permute(block, 2 * k, count) for k in (1, 2, 3)]
    across = dp_permute(block, 1, count)
    rest = [dp_permute(part, 1, count) for part in along_z]
    return [block, across, along_z[0], rest[0], along_z[1], rest[1], along_z[2], rest[2]]


def weight_scratch(blocks):
    pages, rows, wide = blocks[0].shape
    return pltpu.VMEM((pages, len(blocks), rows, wide), blocks[0].dtype)


def assemble(sc, block_refs, scratch):
    count = len(block_refs)
    own = sc[S_DP]
    for k, ref in enumerate(block_refs):
        place = lax.bitwise_xor(own, k) if count > 1 else 0
        scratch[:, place] = ref[...]
    _, _, rows, wide = scratch.shape
    return lambda page: scratch[page].reshape(count * rows, wide)


def emit(sc, page, value, outs, scratch):
    value = value.astype(BF)
    if len(outs) == 1:
        outs[0][page] = value
        return
    keep, give = outs
    scratch[...] = value.reshape(scratch.shape)
    x = sc[S_X]
    for z in range(4):
        keep[page, z] = scratch[2 * z + x]
        give[page, z] = scratch[2 * z + 1 - x]


def grad_outs(pages, rows, wide, count):
    if count != 8:
        return [sds((pages, rows, wide), BF)]
    return [sds((pages, 4, rows // 8, wide), BF)] * 2


def grad_scratch(rows, wide):
    return pltpu.VMEM((8, rows // 8, wide), BF)


def sum_x_kernel(sc, keep, got, own, one, two, three, total):
    total[...] = keep[...].astype(F32) + got[...].astype(F32)
    z = sc[S_Z]
    own[...] = total[:, z]
    one[...] = total[:, lax.bitwise_xor(z, 1)].astype(BF)
    two[...] = total[:, lax.bitwise_xor(z, 2)].astype(BF)
    three[...] = total[:, lax.bitwise_xor(z, 3)].astype(BF)


def add_parts(parts):
    values = [part[...].astype(F32) for part in parts]
    if len(values) == 1:
        return values[0]
    return (values[0] + values[1]) + (values[2] + values[3])


def square_sum(value):
    while value.ndim > 2:
        value = value.reshape((-1,) + value.shape[-1:]) if value.ndim == 3 else value[0]
    rows = jnp.sum(value * value, axis=0, keepdims=True)
    return jnp.sum(rows, axis=1, keepdims=True)


def sum_early_kernel(counts, sc, *refs):
    squares, at, total = refs[-1], sum(counts), jnp.zeros((1, 1), F32)
    first = 0
    for g, count in enumerate(counts):
        value = add_parts(refs[first : first + count])
        first += count
        refs[at + g][...] = value
        total += square_sum(value)
    squares[...] = jnp.broadcast_to(total, (8, 128))


def late_rows(ref):
    half = WIDE // 4
    rows = (ref.shape[0] * 2) // 5
    pages = ref[0 : 2 * rows, :].astype(F32).reshape(2, rows, ref.shape[1])
    patch = jnp.concatenate([ref[2 * rows :, 0:half], ref[2 * rows :, half:]], axis=0).astype(F32)
    return pages, patch


def sum_x_late_kernel(sc, keep, got, keep_patch, got_patch, own, own_patch, one, two, three, total, total_patch):
    total[...] = keep[...].astype(F32) + got[...].astype(F32)
    total_patch[...] = keep_patch[0].astype(F32) + got_patch[0].astype(F32)
    z = sc[S_Z]
    own[...] = total[:, z]
    own_patch[0] = total_patch[z]
    rows, half = own.shape[1], own_patch.shape[2]
    for k, ref in enumerate((one, two, three)):
        to = lax.bitwise_xor(z, k + 1)
        for page in range(2):
            ref[rows * page : rows * (page + 1), :] = total[page, to].astype(BF)
        for page in range(2):
            piece = total_patch[to, rows // 2 * page : rows // 2 * (page + 1), :]
            ref[2 * rows :, half * page : half * (page + 1)] = piece.astype(BF)


def sum_late_kernel(travelled, small_parts, dp, tp, sc, early, own, own_patch, *refs):
    blocks, parts = refs[:travelled], refs[travelled : travelled + small_parts]
    shard, patch_shard, small, shares = refs[travelled + small_parts :]
    value, patch = own[...], own_patch[0]
    if travelled:
        (one, p1), (two, p2), (three, p3) = [late_rows(ref) for ref in blocks]
        value = (value + one) + (two + three)
        patch = (patch + p1) + (p2 + p3)
    shard[...] = value
    patch_shard[0] = patch
    held = add_parts(parts)
    small[...] = held
    row = lax.broadcasted_iota(jnp.int32, (held.shape[0], 1), 0)
    weight = jnp.where(row < 13, (1.0 / (dp * tp)) ** 0.5, (1.0 / dp) ** 0.5)
    held = held * jnp.where(row < held.shape[0] - 1, weight, 0.0)
    total = early[0:1, 0:1] + square_sum(value) + square_sum(patch) + square_sum(held)
    shares[...] = jnp.broadcast_to(total.reshape(1, 1, 1), shares.shape)


def scatter_start(sc, grads):
    count = lax.axis_size("dp")
    if count != 8:
        return [lax.psum_scatter(grads[0].astype(F32), "dp", scatter_dimension=1, tiled=True)]
    keep, give = grads
    got = dp_permute(give, 1, count)
    pages, _, rows, wide = keep.shape
    block = (pages, rows, wide)
    own, one, two, three = call(
        sum_x_kernel, [sds(block, F32)] + [sds(block, BF)] * 3, (sc, keep, got), [pltpu.VMEM(keep.shape, F32)]
    )
    one = dp_permute(one, 2, count)
    two = dp_permute(two, 4, count)
    three = dp_permute(three, 6, count)
    return [own, one, two, three]


def sum_early(sc, started):
    outs = call(
        functools.partial(sum_early_kernel, [len(s) for s in started]),
        [sds(s[0].shape, F32) for s in started] + [sds((8, 128), F32)],
        (sc, *[part for s in started for part in s]),
    )
    return list(outs[:-1]), outs[-1]


def late_start(sc, grads, patch_grads):
    count = lax.axis_size("dp")
    if count != 8:
        return scatter_start(sc, grads) + scatter_start(sc, patch_grads)
    keep, give = grads
    keep_patch, give_patch = patch_grads
    got = dp_permute(give, 1, count)
    got_patch = dp_permute(give_patch, 1, count)
    pages, _, rows, wide = keep.shape
    half = keep_patch.shape[3]
    own, own_patch, *blocks = call(
        sum_x_late_kernel,
        [sds((pages, rows, wide), F32), sds((1, rows, half), F32)] + [sds((5 * rows // 2, wide), BF)] * 3,
        (sc, keep, got, keep_patch, got_patch),
        [pltpu.VMEM(keep.shape, F32), pltpu.VMEM(keep_patch.shape[1:], F32)],
    )
    return [own, own_patch] + [dp_permute(b, 2 * k + 2, count) for k, b in enumerate(blocks)]


def sum_late(sc, early, started, small_parts, dp, tp):
    return call(
        functools.partial(sum_late_kernel, len(started) - 2, len(small_parts), dp, tp),
        [sds(a.shape, F32) for a in (started[0], started[1], small_parts[0])] + [sds((dp * tp, 8, 128), F32)],
        (sc, early, *started, *small_parts),
    )


def small_start(value):
    count = lax.axis_size("dp")
    if count != 8:
        return [lax.psum(value, "dp")]
    value = value + dp_permute(value, 1, count)
    return [value] + [dp_permute(value, 2 * k, count) for k in (1, 2, 3)]


def tensor_gather(value):
    across = tp_permute(value, 2)
    return [value, tp_permute(value, 1), across, tp_permute(across, 1)]


def tensor_sum(keep, send):
    pair = (keep.astype(F32) + tp_permute(send, 1).astype(F32)).astype(BF)
    own = pair.astype(F32) + tp_permute(pair, 2).astype(F32)
    return own, tp_permute(own, 1)


def split_dot(dot, left, right, parts):
    total = None
    for _ in range(parts):
        part = right.astype(BF)
        right = right - part.astype(F32)
        value = dot(left, part)
        total = value if total is None else total + value
    return total


def spread_matrix(dtype):
    j = lax.broadcasted_iota(jnp.int32, (ROWS, 384), 0)
    k = lax.broadcasted_iota(jnp.int32, (ROWS, 384), 1)
    tall = lax.shift_right_logical(j * 4682, 16)
    place = SPAN * (GRID - 1 - tall) + (GRID - 1) - (j - GRID * tall)
    return jnp.where((place == k) & (j < NPATCH), 1.0, 0.0).astype(dtype)


def table_kernel(sc, table, bias, stage):
    spread = spread_matrix(BF)
    row16 = lax.broadcasted_iota(jnp.int32, (16, WIDE), 0)
    i = lax.broadcasted_iota(jnp.int32, (ROWS, ROWS), 0)
    j = lax.broadcasted_iota(jnp.int32, (ROWS, ROWS), 1)

    @pl.loop(0, table.shape[0])
    def _(h):
        held = table[pl.ds(h, 1), :]
        line = jnp.concatenate([held, jnp.zeros((1, WIDE - NREL), F32)], axis=1)
        wide = jnp.broadcast_to(line, (16, WIDE))
        shifted = wide
        for c in range(1, GRID):
            shifted = jnp.where(row16 == c, pltpu.roll(wide, WIDE - c, 1), shifted)
        stage[...] = jnp.zeros(stage.shape, F32)
        for r in range(GRID):
            turned = shifted if r == 0 else pltpu.roll(shifted, WIDE - SPAN * r, 1)
            stage[GRID * r : GRID * r + 16, :] = turned[:, 0:384]
        inner = split_dot(lambda one, two: dot_nt(two, one), spread, stage[...], 3)
        to_all = held[:, NREL - 3 : NREL - 2]
        to_class = held[:, NREL - 2 : NREL - 1]
        corner = held[:, NREL - 1 : NREL]
        edge = jnp.where(j == NPATCH, corner, to_all)
        inner = jnp.where(i == NPATCH, edge, jnp.where(j == NPATCH, to_class, inner))
        inner = jnp.where(i > NPATCH, 0.0, inner)
        bias[h] = jnp.where(j > NPATCH, MASKED, inner)


def covered_rows(sc, places, image):
    slots = places.shape[1]
    patch = lax.broadcasted_iota(jnp.int32, (NPATCH, slots), 0)
    slot = lax.broadcasted_iota(jnp.int32, (NPATCH, slots), 1)
    hit = (patch == places[pl.ds(image, 1), :]) & (slot < sc[S_COUNT0 + image])
    return jnp.max(jnp.where(hit, 1.0, 0.0), axis=1, keepdims=True)


def picks(places, image, slots):
    row = lax.broadcasted_iota(jnp.int32, (slots, ROWS), 1)
    return row == places[image * slots : (image + 1) * slots, :]


def rows_of(image):
    return pl.ds(pl.multiple_of(image * ROWS, 16), ROWS)


def heads_of(array, image, h, first=0):
    return array[rows_of(image), first + HD * h : first + HD * (h + 1)]


def order_quarters(sc, quarters, scratch):
    for k, ref in enumerate(quarters):
        scratch[lax.bitwise_xor(sc[S_TP], k)] = ref[...]


def patch_kernel(blocks, sc, *refs):
    page = assemble(sc, refs[:blocks], refs[-1])
    refs[blocks][...] = page(0)


def attend_kernel(blocks, sc, images, places, vectors, biases, bias, *refs):
    quarters, weight_refs = refs[:4], refs[4 : 4 + blocks]
    stream_ref, qk_ref, v_ref, heads_ref, keep, send, weights, term, patch = refs[4 + blocks :]
    share = v_ref.shape[1]
    page = assemble(sc, weight_refs, weights)
    order_quarters(sc, quarters, patch)
    final = vectors.shape[0] - 5

    @pl.loop(0, 2)
    def _(b):
        held = images[b]
        covered = covered_rows(sc, places, b)
        embedded = jnp.concatenate([dot_nn(held, patch[k]) for k in range(4)], axis=1)
        embedded = embedded + vectors[final + 2 : final + 3, :]
        embedded = embedded * (1.0 - covered) + vectors[final + 4 : final + 5, :] * covered
        stream_ref[b, 192:ROWS, :] = jnp.zeros((ROWS - 192, WIDE), F32)
        stream_ref[b, 0:NPATCH, :] = embedded
        stream_ref[b, NPATCH : NPATCH + 1, :] = vectors[final + 3 : final + 4, :]

    unit, _ = norm_parts(stream_ref[...].reshape(2 * ROWS, WIDE))
    entered = (unit * vectors[0:1, :] + vectors[1:2, :]).astype(BF)
    joined = dot_nn(entered, page(0))
    shift = jnp.concatenate([biases[0, 0:1, :], jnp.zeros((1, share), F32)], axis=1)
    qk_ref[...] = (joined + shift).astype(BF)
    second = page(1)
    v_ref[...] = (dot_nn(entered, second[:, 0:share]) + biases[0, 1:2, :]).astype(BF)

    @pl.loop(0, 2)
    def _(b):
        for h in range(share // HD):
            scores = dot_nt(heads_of(qk_ref, b, h), heads_of(qk_ref, b, h, share)) * 0.125 + bias[h]
            scores = jnp.exp(scores - jnp.max(scores, axis=1, keepdims=True))
            soft = scores / jnp.sum(scores, axis=1, keepdims=True)
            heads_ref[rows_of(b), HD * h : HD * (h + 1)] = dot_nn(soft.astype(BF), heads_of(v_ref, b, h)).astype(BF)

    term[...] = dot_nt(heads_ref[...], second[:, share:]).astype(BF).reshape(term.shape)
    keep[...] = term[sc[S_CORE]]
    send[...] = term[1 - sc[S_CORE]]


def add_branch(sc, out, base, own, other, gamma, shift):
    core = sc[S_CORE]
    out[core] = base[core] + gamma * (own[...] + shift)
    out[1 - core] = base[1 - core] + gamma * (other[...] + shift)


def feed_kernel(blocks, sc, stream, own, other, vectors, biases, *refs):
    weight_refs = refs[:blocks]
    middle, pre_ref, active_ref, keep, send, weights, term = refs[blocks:]
    page = assemble(sc, weight_refs, weights)
    add_branch(sc, middle, stream, own, other, vectors[3:4, :], vectors[2:3, :])
    unit, _ = norm_parts(middle[...].reshape(2 * ROWS, WIDE))
    entered = (unit * vectors[4:5, :] + vectors[5:6, :]).astype(BF)
    total = None
    half = WIDE // 2
    for g in range(2):
        shift = jnp.concatenate([biases[0, 2 + 2 * g : 3 + 2 * g, :], biases[0, 3 + 2 * g : 4 + 2 * g, :]], axis=1)
        pre = dot_nn(entered, page(g)) + shift
        pre_ref[:, half * g : half * (g + 1)] = pre
        active = (0.5 * pre * (1.0 + lax.erf(pre * 0.7071067811865476))).astype(BF)
        active_ref[:, half * g : half * (g + 1)] = active
        part = dot_nt(active, page(2 + g))
        total = part if total is None else total + part
    term[...] = total.astype(BF).reshape(term.shape)
    keep[...] = term[sc[S_CORE]]
    send[...] = term[1 - sc[S_CORE]]


def logit_kernel(blocks, sc, middle, own, other, vectors, places, codes, logit_bias, *refs):
    stream, picked_ref, logits_ref, stats, weights, more_weights = refs[2 * blocks :]
    pages = (assemble(sc, refs[:blocks], weights)(0), assemble(sc, refs[blocks : 2 * blocks], more_weights)(0))
    final = vectors.shape[0] - 5
    slots = places.shape[0] // 2
    add_branch(sc, stream, middle, own, other, vectors[7:8, :], vectors[6:7, :])
    wanted = []
    for b in range(2):
        unit, _ = norm_parts(stream[b])
        closing = (unit * vectors[final : final + 1, :] + vectors[final + 1 : final + 2, :]).astype(BF)
        hit = picks(places, b, slots)
        picked_ref[b * slots : (b + 1) * slots, :] = dot_nn(jnp.where(hit, 1.0, 0.0).astype(BF), closing).astype(BF)
        found = jnp.where(hit[:, 0:NPATCH], codes[b : b + 1, :].astype(F32), 0.0)
        wanted.append(jnp.sum(found, axis=1, keepdims=True))
    wanted = jnp.concatenate(wanted, axis=0)
    first = 0
    for page in pages:
        last = first + page.shape[1]
        logits_ref[:, first:last] = dot_nn(picked_ref[...], page) + logit_bias[:, first:last]
        first = last
    logits = logits_ref[...]
    share = logits.shape[1]
    first = (sc[S_TP] * share).astype(F32)
    column = lax.broadcasted_iota(jnp.int32, logits.shape, 1).astype(F32)
    peak = jnp.max(logits, axis=1, keepdims=True)
    summed = jnp.sum(jnp.exp(logits - peak), axis=1, keepdims=True)
    chosen = jnp.sum(jnp.where(column == wanted - first, logits, 0.0), axis=1, keepdims=True)
    lane = lax.broadcasted_iota(jnp.int32, stats.shape, 1)
    stats[...] = jnp.where(lane == 0, peak, jnp.where(lane == 1, summed, jnp.where(lane == 2, chosen, wanted)))


def join_stats(one, two):
    peak = jnp.maximum(one[:, 0:1], two[:, 0:1])
    summed = one[:, 1:2] * jnp.exp(one[:, 0:1] - peak) + two[:, 1:2] * jnp.exp(two[:, 0:1] - peak)
    return peak, summed, one[:, 2:3] + two[:, 2:3]


def stats_kernel(sc, one, two, out):
    peak, summed, chosen = join_stats(one[...], two[...])
    lane = lax.broadcasted_iota(jnp.int32, out.shape, 1)
    out[...] = jnp.where(lane == 0, peak, jnp.where(lane == 1, summed, jnp.where(lane == 2, chosen, one[:, 3:4])))


def loss_kernel(blocks, sc, one, two, logits_ref, *refs):
    grad_ref, shift_ref, loss_ref, keep, send, weights, more_weights, term = refs[2 * blocks :]
    pages = (assemble(sc, refs[:blocks], weights)(0), assemble(sc, refs[blocks : 2 * blocks], more_weights)(0))
    logits = logits_ref[...]
    slots = logits.shape[0] // 2
    share = logits.shape[1]
    peak, summed, chosen = join_stats(one[...], two[...])
    logsum = peak + jnp.log(summed)
    slot = lax.broadcasted_iota(jnp.int32, (2 * slots, 1), 0)
    live = jnp.where(
        slot < slots,
        jnp.where(slot < sc[S_COUNT0], 1.0, 0.0),
        jnp.where(slot - slots < sc[S_COUNT1], 1.0, 0.0),
    )
    total = jnp.full((2 * slots, 1), sc[S_TOTAL], jnp.int32).astype(F32)
    loss_ref[...] = jnp.broadcast_to(column_sum(live * (logsum - chosen)), loss_ref.shape)
    first = (sc[S_TP] * share).astype(F32)
    column = lax.broadcasted_iota(jnp.int32, logits.shape, 1).astype(F32)
    matched = jnp.where(column == one[:, 3:4] - first, 1.0, 0.0)
    grad = ((live / total) * (jnp.exp(logits - logsum) - matched)).astype(BF)
    grad_ref[...] = grad
    shift_ref[...] = column_sum(grad.astype(F32))
    wide = pages[0].shape[1]
    total = dot_nt(grad[:, :wide], pages[0]) + dot_nt(grad[:, wide:], pages[1])
    term[...] = total.astype(BF).reshape(term.shape)
    keep[...] = term[sc[S_CORE]]
    send[...] = term[1 - sc[S_CORE]]


def code_grad_kernel(first, wide, sc, picked, grad, *refs):
    outs, scratch = refs[:-1], refs[-1]
    emit(sc, 0, dot_tn(picked[...], grad[:, first : first + wide]), outs, scratch)


def branch_back(sc, gated_ref, sums, first, upstream, own, other, gamma, shift):
    core = sc[S_CORE]
    gamma_sum = column_sum(upstream[core] * (own[...] + shift)) + column_sum(
        upstream[1 - core] * (other[...] + shift)
    )
    sums[first + 1 : first + 2, :] = gamma_sum
    gated = upstream[...].reshape(2 * ROWS, WIDE) * gamma
    sums[first : first + 1, :] = column_sum(gated)
    gated_ref[...] = gated.astype(BF)


def feed_back_kernel(blocks, sc, own, other, places, stream, branch_own, branch_other, vectors, pre_ref, *refs):
    weight_refs = refs[:blocks]
    upstream, gated_ref, grad_pre_ref, sums, keep, send, weights, term, picked = refs[blocks:]
    page = assemble(sc, weight_refs, weights)
    core = sc[S_CORE]
    final = vectors.shape[0] - 5
    slots = places.shape[0] // 2
    picked[core] = own[...]
    picked[1 - core] = other[...]
    gain_sum = jnp.zeros((1, WIDE), F32)
    shift_sum = jnp.zeros((1, WIDE), F32)
    for b in range(2):
        hit = jnp.where(picks(places, b, slots), 1.0, 0.0).astype(BF)
        closing = split_dot(dot_tn, hit, picked[b], 3)
        unit, inverse = norm_parts(stream[b])
        gain_sum += column_sum(closing * unit)
        shift_sum += column_sum(closing)
        upstream[b] = norm_back(closing, vectors[final : final + 1, :], unit, inverse)
    sums[0:1, :] = gain_sum
    sums[1:2, :] = shift_sum
    branch_back(sc, gated_ref, sums, 2, upstream, branch_own, branch_other, vectors[7:8, :], vectors[6:7, :])
    gated = gated_ref[...]
    total = None
    half = WIDE // 2
    for g in range(2):
        pre = pre_ref[:, half * g : half * (g + 1)]
        grad_active = dot_nn(gated, page(2 + g))
        slope = 0.5 * (1.0 + lax.erf(pre * 0.7071067811865476)) + pre * (
            jnp.exp(-0.5 * pre * pre) * 0.3989422804014327
        )
        grad_pre = (grad_active * slope).astype(BF)
        grad_pre_ref[:, half * g : half * (g + 1)] = grad_pre
        sums[4:5, half * g : half * (g + 1)] = column_sum(grad_pre.astype(F32))
        part = dot_nt(grad_pre, page(g))
        total = part if total is None else total + part
    term[...] = total.astype(BF).reshape(term.shape)
    keep[...] = term[core]
    send[...] = term[1 - core]


def feed_grad_kernel(sc, middle, vectors, grad_pre, gated, active, *refs):
    outs, scratch, held = refs[:-2], refs[-2], refs[-1]
    half = WIDE // 2
    unit, _ = norm_parts(middle[...].reshape(2 * ROWS, WIDE))
    entered = (unit * vectors[4:5, :] + vectors[5:6, :]).astype(BF)
    held[...] = entered

    @pl.loop(0, 2)
    def _(g):
        columns = pl.ds(pl.multiple_of(half * g, 128), half)
        emit(sc, g, dot_tn(held[...], grad_pre[:, columns]), outs, scratch)
        emit(sc, 2 + g, dot_tn(gated[...], active[:, columns]), outs, scratch)


def attend_back_kernel(
    blocks, sc, own, other, upstream, middle, branch_own, branch_other, vectors, qk, v, bias, *refs
):
    weight_refs = refs[:blocks]
    passed, gated_ref, grad_qk, grad_v, sums, table_sums, keep, send = refs[blocks : blocks + 8]
    weights, term, grad_heads, stage, together = refs[blocks + 8 :]
    page = assemble(sc, weight_refs, weights)
    core = sc[S_CORE]
    share = v.shape[1]
    gain = vectors[4:5, :]
    gain_sum = jnp.zeros((1, WIDE), F32)
    shift_sum = jnp.zeros((1, WIDE), F32)
    for image, arrived in ((core, own), (1 - core, other)):
        grad = arrived[...]
        unit, inverse = norm_parts(middle[image])
        gain_sum += column_sum(grad * unit)
        shift_sum += column_sum(grad)
        passed[image] = upstream[image] + norm_back(grad, gain, unit, inverse)
    sums[0:1, :] = gain_sum
    sums[1:2, :] = shift_sum
    branch_back(sc, gated_ref, sums, 2, passed, branch_own, branch_other, vectors[3:4, :], vectors[2:3, :])
    second = page(1)
    grad_heads[...] = dot_nn(gated_ref[...], second[:, share:]).astype(BF)
    spread = spread_matrix(BF)
    lane = lax.broadcasted_iota(jnp.int32, (1, WIDE), 1)
    row16 = lax.broadcasted_iota(jnp.int32, (16, WIDE), 0)
    i = lax.broadcasted_iota(jnp.int32, (ROWS, ROWS), 0)
    j = lax.broadcasted_iota(jnp.int32, (ROWS, ROWS), 1)

    for b in range(2):
        rows = rows_of(b)
        for h in range(share // HD):
            queries, keys, values = heads_of(qk, b, h), heads_of(qk, b, h, share), heads_of(v, b, h)
            scores = dot_nt(queries, keys) * 0.125 + bias[h]
            scores = jnp.exp(scores - jnp.max(scores, axis=1, keepdims=True))
            soft = scores / jnp.sum(scores, axis=1, keepdims=True)
            grad_out = heads_of(grad_heads, b, h)
            grad_v[rows, HD * h : HD * (h + 1)] = dot_tn(soft.astype(BF), grad_out).astype(BF)
            grad_soft = dot_nt(grad_out, values)
            grad_scores = soft * (grad_soft - jnp.sum(soft * grad_soft, axis=1, keepdims=True))
            grad_scores = grad_scores.astype(BF)
            grad_qk[rows, HD * h : HD * (h + 1)] = (dot_nn(grad_scores, keys) * 0.125).astype(BF)
            grad_qk[rows, share + HD * h : share + HD * (h + 1)] = (dot_tn(grad_scores, queries) * 0.125).astype(BF)
            together[b, h] = grad_scores

    for h in range(share // HD):
        stage[...] = dot_nn(together[0, h], spread) + dot_nn(together[1, h], spread)
        lined = jnp.zeros((16, WIDE), F32)
        for r in range(GRID):
            piece = jnp.concatenate([stage[GRID * r : GRID * r + 16, :], jnp.zeros((16, WIDE - 384), F32)], axis=1)
            lined += piece if r == 0 else pltpu.roll(piece, SPAN * r, 1)
        folded = jnp.where(row16 == 0, lined, 0.0)
        for c in range(1, GRID):
            folded += pltpu.roll(jnp.where(row16 == c, lined, 0.0), c, 1)
        line = column_sum(folded)
        on_row, on_column = i == NPATCH, j == NPATCH
        added = together[0, h].astype(F32) + together[1, h].astype(F32)
        to_all = jnp.sum(jnp.where(on_row & (j < NPATCH), added, 0.0))
        to_class = jnp.sum(jnp.where(on_column & (i < NPATCH), added, 0.0))
        corner = jnp.sum(jnp.where(on_row & on_column, added, 0.0))
        line = jnp.where(lane == NREL - 3, to_all, line)
        line = jnp.where(lane == NREL - 2, to_class, line)
        line = jnp.where(lane == NREL - 1, corner, line)
        table_sums[pl.ds(h, 1), :] = line

    sums[4:5, 0:share] = column_sum(grad_qk[:, 0:share].astype(F32))
    sums[4:5, share : 2 * share] = column_sum(grad_v[...].astype(F32))
    sums[4:5, 2 * share :] = jnp.zeros((1, WIDE - 2 * share), F32)
    total = dot_nt(grad_qk[...], page(0)) + dot_nt(grad_v[...], second[:, 0:share])
    term[...] = total.astype(BF).reshape(term.shape)
    keep[...] = term[core]
    send[...] = term[1 - core]


def attend_grad_kernel(sc, stream, vectors, grad_qk, grad_v, gated, heads, *refs):
    outs, scratch = refs[:-1], refs[-1]
    unit, _ = norm_parts(stream[...].reshape(2 * ROWS, WIDE))
    entered = (unit * vectors[0:1, :] + vectors[1:2, :]).astype(BF)
    emit(sc, 0, dot_tn(entered, grad_qk[...]), outs, scratch)
    pair = jnp.concatenate([dot_tn(entered, grad_v[...]), dot_tn(gated[...], heads[...])], axis=1)
    emit(sc, 1, pair, outs, scratch)


def embed_back_kernel(sc, own, other, passed, stream, vectors, images, places, feed_sums, attend_sums, table_sums, logit_sums, loss, *refs):
    small, outs = refs[0], refs[1:-3]
    scratch, grads, quarters = refs[-3:]
    core = sc[S_CORE]
    gain = vectors[0:1, :]
    zero = jnp.zeros((1, WIDE), F32)
    gain_sum, shift_sum = zero, zero
    for image, arrived in ((core, own), (1 - core, other)):
        grad = arrived[...]
        unit, inverse = norm_parts(stream[image])
        gain_sum += column_sum(grad * unit)
        shift_sum += column_sum(grad)
        grads[image] = passed[image] + norm_back(grad, gain, unit, inverse)
    patch_sum, class_sum, mask_sum = zero, zero, zero
    quarter = WIDE // 4
    for b in range(2):
        grad = grads[b, 0:NPATCH, :]
        covered = covered_rows(sc, places, b)
        through = grad * (1.0 - covered)
        patch_sum += column_sum(through)
        mask_sum += column_sum(grad * covered)
        class_sum += grads[b, NPATCH : NPATCH + 1, :]
        through = through.astype(BF)
        for k in range(4):
            quarters[k, b] = through[:, quarter * k : quarter * (k + 1)]
    mine = sc[S_TP]
    emit(sc, 0, dot_tn(images[0], quarters[mine, 0]) + dot_tn(images[1], quarters[mine, 1]), outs, scratch)
    small[...] = jnp.zeros(small.shape, F32)
    small[0:1, :] = gain_sum
    small[1:2, :] = shift_sum
    small[2:4, :] = attend_sums[2:4, :]
    small[4:6, :] = attend_sums[0:2, :]
    small[6:8, :] = feed_sums[2:4, :]
    small[8:10, :] = feed_sums[0:2, :]
    small[10:11, :] = patch_sum
    small[11:12, :] = class_sum
    small[12:13, :] = mask_sum
    small[13:14, :] = attend_sums[4:5, :]
    small[14:15, :] = feed_sums[4:5, :]
    heads = table_sums.shape[0]
    small[15 : 15 + heads, :] = table_sums[...]
    first = 15 + heads
    left = logit_sums.shape[1]
    row = 0
    while left > 0:
        take = min(left, WIDE)
        small[first + row : first + row + 1, 0:take] = logit_sums[:, row * WIDE : row * WIDE + take]
        left -= take
        row += 1
    small[first + row : first + row + 1, 0:128] = loss[...]


def clip_of(spread):
    norm = jnp.sqrt(jnp.sum(spread[...], axis=0)[0:1, 0:1])
    return norm, jnp.minimum(1.0, CLIP_NORM / (norm + 1e-06))


def adam(master, first_old, root_old, gradient, fix, decay):
    clip, first_fix, second_fix = fix
    clipped = gradient * clip
    first = BETA_ONE * first_old + (1.0 - BETA_ONE) * clipped
    root = jnp.sqrt(BETA_TWO * root_old * root_old + (1.0 - BETA_TWO) * clipped * clipped)
    direction = first / first_fix / (root / second_fix + ADAM_EPS) + decay * master
    return master - LEARN_RATE * direction, first, root


def adam_matrix_kernel(
    sc, fix_ref, spread, in_w, in_m, out_w, out_m, patch_w, patch_m, first, feed, patch0, patch1, patch2, patch3,
    in_master, in_state, out_master, out_state, patch_master, patch_state, patch,
):
    fix = (clip_of(spread)[1], fix_ref[0], fix_ref[1])
    order_quarters(sc, (patch0, patch1, patch2, patch3), patch)
    share = in_w.shape[3]
    half = 2 * share

    def into(j, gradient):
        in_master[0, j], in_state[0, 0, j], in_state[1, 0, j] = adam(
            in_w[0, j], in_m[0, 0, j], in_m[1, 0, j], gradient, fix, WEIGHT_DECAY
        )

    def outof(j, gradient):
        out_master[0, j], out_state[0, 0, j], out_state[1, 0, j] = adam(
            out_w[0, j], out_m[0, 0, j], out_m[1, 0, j], gradient.T, fix, WEIGHT_DECAY
        )

    into(0, first[0, :, 0:share])
    into(1, first[0, :, share:half])
    into(2, first[1, :, 0:share])
    outof(0, first[1, :, share:half])
    for g in range(2):
        for k in range(2):
            into(3 + 2 * g + k, feed[g, :, share * k : share * (k + 1)])
            outof(1 + 2 * g + k, feed[2 + g, :, share * k : share * (k + 1)])
    for g in range(4):
        columns = slice(g * share, (g + 1) * share)
        patch_master[:, columns], patch_state[0, :, columns], patch_state[1, :, columns] = adam(
            patch_w[:, columns], patch_m[0, :, columns], patch_m[1, :, columns], patch[g, 0], fix, WEIGHT_DECAY
        )


def adam_code_kernel(pieces, sc, fix_ref, spread, code_w, code_m, *refs):
    fix = (clip_of(spread)[1], fix_ref[0], fix_ref[1])
    grads = refs[:pieces]
    code_master, code_state = refs[pieces:]
    first = 0
    for grad in grads:
        columns = slice(first, first + grad.shape[2])
        first += grad.shape[2]
        code_master[:, columns], code_state[0, :, columns], code_state[1, :, columns] = adam(
            code_w[:, columns], code_m[0, :, columns], code_m[1, :, columns], grad[0], fix, WEIGHT_DECAY
        )


def adam_small_kernel(
    sc, fix_ref, spread, small, bias_w, bias_m, vec_w, vec_m, table_w, table_m, logit_w, logit_m,
    bias_master, bias_state, vec_master, vec_state, table_master, table_state, logit_master, logit_state, loss_out, norm_out,
):
    norm, clip = clip_of(spread)
    fix = (clip, fix_ref[0], fix_ref[1])
    norm_out[0] = jnp.sum(norm)
    loss = small[small.shape[0] - 1 : small.shape[0], 0:1] / jnp.full((1, 1), sc[S_TOTAL], jnp.int32).astype(F32)
    loss_out[0] = jnp.sum(loss)
    share = bias_w.shape[2]
    for j in range(6):
        row, k = (13, j) if j < 2 else (14, j - 2)
        gradient = small[row : row + 1, share * k : share * (k + 1)]
        bias_master[j], bias_state[0, j], bias_state[1, j] = adam(
            bias_w[j], bias_m[0, j], bias_m[1, j], gradient, fix, 0.0
        )
    vec_master[...], vec_state[:, 0, :], vec_state[:, 1, :] = adam(
        vec_w[...], vec_m[:, 0, :], vec_m[:, 1, :], small[0:13, :], fix, 0.0
    )
    heads = table_w.shape[0]
    table_master[...], table_state[:, 0, :], table_state[:, 1, :] = adam(
        table_w[...], table_m[:, 0, :], table_m[:, 1, :], small[15 : 15 + heads, 0:NREL], fix, 0.0
    )
    first = 15 + heads
    share = logit_w.shape[1]
    gradient = jnp.concatenate(
        [small[first + k : first + k + 1, 0 : min(WIDE, share - k * WIDE)] for k in range(-(-share // WIDE))], axis=1
    )
    logit_master[...], logit_state[0:1, :], logit_state[1:2, :] = adam(
        logit_w[...], logit_m[0:1, :], logit_m[1:2, :], gradient, fix, 0.0
    )


def local(
    images, mask_places, mask_counts, codes, step_count,
    in_weights, in_moments, out_weights, out_moments, patch_weight, patch_moments,
    code_weight, code_moments, in_biases, bias_moments, vectors, vector_moments,
    rel_table, table_moments, logit_bias, logit_moments,
):
    dp = lax.axis_size("dp")
    tp = lax.axis_size("tensor")
    dp_index = lax.axis_index("dp").astype(jnp.int32)
    tp_index = lax.axis_index("tensor").astype(jnp.int32)
    share = in_weights.shape[3]
    code_share = code_weight.shape[1]
    slots = mask_places.shape[1]
    heads = rel_table.shape[0]
    own_counts = lax.dynamic_slice_in_dim(mask_counts, dp_index * 2, 2)
    total_count = jnp.sum(mask_counts)
    sc = jnp.stack(
        [dp_index, tp_index, tp_index & 1, dp_index & 1, dp_index >> 1, own_counts[0], own_counts[1], total_count]
    )

    into = in_weights[0].astype(BF)
    outof = out_weights[0].astype(BF).transpose(0, 2, 1)
    quarter = WIDE // tp
    patch_group = lax.dynamic_slice_in_dim(patch_weight, tp_index * quarter, quarter, 1).astype(BF)[None]

    def pair(one, two):
        return jnp.concatenate([one, two], axis=-1)

    first_group = jnp.stack(
        [pair(into[:, 0], into[:, 1]), pair(into[:, 2], outof[0])]
    )
    second_group = jnp.stack(
        [pair(into[:, 3], into[:, 4]), pair(into[:, 5], into[:, 6]), pair(outof[1], outof[2]), pair(outof[3], outof[4])]
    )
    code_cut = CODE_GROUPS[0] * code_share // sum(CODE_GROUPS)
    patch_blocks = gather_blocks(patch_group)
    first_blocks = gather_blocks(first_group)
    second_blocks = gather_blocks(second_group)
    code_blocks = gather_blocks(code_weight[:, :code_cut].astype(BF)[None])
    more_blocks = gather_blocks(code_weight[:, code_cut:].astype(BF)[None])
    nb = len(first_blocks)
    (patch_own,) = call(
        functools.partial(patch_kernel, nb), [sds((WIDE, quarter), BF)], (sc, *patch_blocks),
        [weight_scratch(patch_blocks)],
    )
    patch_quarters = tensor_gather(patch_own)

    (bias,) = call(table_kernel, [sds((heads, ROWS, ROWS), F32)], (sc, rel_table), [pltpu.VMEM((ROWS, 384), F32)])
    stacked = sds((2, ROWS, WIDE), F32)
    term_outs = [sds((ROWS, WIDE), BF)] * 2
    term_scratch = pltpu.VMEM((2, ROWS, WIDE), BF)
    places_column = mask_places.reshape(2 * slots, 1)
    matmul_flops = 2 * 2 * ROWS * WIDE

    stream, qk, v, attended, keep, send = call(
        functools.partial(attend_kernel, nb),
        [stacked, sds((2 * ROWS, 2 * share), BF), sds((2 * ROWS, share), BF), sds((2 * ROWS, share), BF)] + term_outs,
        (sc, images, mask_places, vectors, in_biases, bias, *patch_quarters, *first_blocks),
        [weight_scratch(first_blocks), term_scratch, pltpu.VMEM((4, WIDE, quarter), BF)],
        matmul_flops * 2 * WIDE,
    )
    attend_own, attend_other = tensor_sum(keep, send)
    middle, pre, active, keep, send = call(
        functools.partial(feed_kernel, nb),
        [stacked, sds((2 * ROWS, WIDE), F32), sds((2 * ROWS, WIDE), BF)] + term_outs,
        (sc, stream, attend_own, attend_other, vectors, in_biases, *second_blocks),
        [weight_scratch(second_blocks), term_scratch],
        matmul_flops * 2 * WIDE,
    )
    feed_own, feed_other = tensor_sum(keep, send)
    last, picked, logits, stats = call(
        functools.partial(logit_kernel, nb),
        [stacked, sds((2 * slots, WIDE), BF), sds((2 * slots, code_share), F32), sds((2 * slots, 128), F32)],
        (sc, middle, feed_own, feed_other, vectors, places_column, codes, logit_bias.reshape(1, -1), *code_blocks, *more_blocks),
        [weight_scratch(code_blocks), weight_scratch(more_blocks)],
        matmul_flops * 2 * WIDE,
    )
    (stats,) = call(stats_kernel, [sds(stats.shape, F32)], (sc, stats, tp_permute(stats, 1)))
    other_stats = tp_permute(stats, 2)
    slot_outs = [sds((slots, WIDE), BF)] * 2
    grad_logits, logit_sums, loss, keep, send = call(
        functools.partial(loss_kernel, nb),
        [sds((2 * slots, code_share), BF), sds((1, code_share), F32), sds((1, 128), F32)] + slot_outs,
        (sc, stats, other_stats, logits, *code_blocks, *more_blocks),
        [weight_scratch(code_blocks), weight_scratch(more_blocks), pltpu.VMEM((2, slots, WIDE), BF)],
        matmul_flops * 2 * WIDE,
    )
    picked_own, picked_other = tensor_sum(keep, send)
    code_parts = []
    first = 0
    for wide in CODE_PIECES:
        wide = wide * code_share // sum(CODE_PIECES)
        grads = call(
            functools.partial(code_grad_kernel, first, wide),
            grad_outs(1, WIDE, wide, dp),
            (sc, picked, grad_logits),
            [grad_scratch(WIDE, wide)],
            2 * 2 * slots * WIDE * wide,
        )
        first += wide
        code_parts.append(scatter_start(sc, grads))

    upstream, gated, grad_pre, feed_sums, keep, send = call(
        functools.partial(feed_back_kernel, nb),
        [stacked, sds((2 * ROWS, WIDE), BF), sds((2 * ROWS, WIDE), BF), sds((8, WIDE), F32)] + term_outs,
        (sc, picked_own, picked_other, places_column, last, feed_own, feed_other, vectors, pre, *second_blocks),
        [weight_scratch(second_blocks), term_scratch, pltpu.VMEM((2, slots, WIDE), F32)],
        matmul_flops * 2 * WIDE,
    )
    feed_in_own, feed_in_other = tensor_sum(keep, send)
    pair_scratch = [grad_scratch(WIDE, 2 * share)]
    feed_part = scatter_start(
        sc,
        call(
            feed_grad_kernel, grad_outs(4, WIDE, 2 * share, dp),
            (sc, middle, vectors, grad_pre, gated, active),
            pair_scratch + [pltpu.VMEM((2 * ROWS, WIDE), BF)], 2 * matmul_flops * WIDE,
        ),
    )
    passed, gated, grad_qk, grad_v, attend_sums, table_sums, keep, send = call(
        functools.partial(attend_back_kernel, nb),
        [
            stacked, sds((2 * ROWS, WIDE), BF), sds((2 * ROWS, 2 * share), BF), sds((2 * ROWS, share), BF),
            sds((8, WIDE), F32), sds((heads, WIDE), F32),
        ]
        + term_outs,
        (sc, feed_in_own, feed_in_other, upstream, middle, attend_own, attend_other, vectors, qk, v, bias, *first_blocks),
        [
            weight_scratch(first_blocks), term_scratch, pltpu.VMEM((2 * ROWS, share), BF),
            pltpu.VMEM((ROWS, 384), F32), pltpu.VMEM((2, heads, ROWS, ROWS), BF),
        ],
        matmul_flops * 2 * WIDE,
    )
    attend_in_own, attend_in_other = tensor_sum(keep, send)
    first_grads = call(
        attend_grad_kernel, grad_outs(2, WIDE, 2 * share, dp),
        (sc, stream, vectors, grad_qk, grad_v, gated, attended), pair_scratch, matmul_flops * WIDE,
    )
    small_rows = 15 + heads + -(-code_share // WIDE) + 1
    embed_outs = call(
        embed_back_kernel,
        [sds((small_rows, WIDE), F32)] + grad_outs(1, WIDE, quarter, dp),
        (
            sc, attend_in_own, attend_in_other, passed, stream, vectors, images, mask_places,
            feed_sums, attend_sums, table_sums, logit_sums, loss,
        ),
        [grad_scratch(WIDE, quarter), pltpu.VMEM((2, ROWS, WIDE), F32), pltpu.VMEM((4, 2, NPATCH, quarter), BF)],
        matmul_flops * WIDE,
    )
    late_part = late_start(sc, first_grads, embed_outs[1:])
    small_part = small_start(embed_outs[0])
    early, squares = sum_early(sc, [*code_parts, feed_part])
    first_shard, patch_shard, small, shares = sum_late(sc, squares, late_part, small_part, dp, tp)
    spread = lax.all_to_all(shares, ("dp", "tensor"), 0, 0)
    patch_shards = tensor_gather(patch_shard)
    step_number = step_count[0].astype(F32)
    fix = jnp.stack([1.0 - jnp.power(BETA_ONE, step_number), jnp.sqrt(1.0 - jnp.power(BETA_TWO, step_number))])

    def like(array):
        return sds(array.shape, F32)

    in_w, in_m = in_weights.transpose(0, 2, 1, 3), in_moments.transpose(0, 1, 3, 2, 4)
    in_master, in_state, out_master, out_state, patch_master, patch_state = call(
        adam_matrix_kernel,
        [like(a) for a in (in_w, in_m, out_weights, out_moments, patch_weight, patch_moments)],
        (
            sc, fix, spread, in_w, in_m, out_weights, out_moments, patch_weight, patch_moments,
            first_shard, early[-1], *patch_shards,
        ),
        [pltpu.VMEM((4,) + patch_shard.shape, F32)],
        scalars=2,
    )
    code_master, code_state = call(
        functools.partial(adam_code_kernel, len(code_parts)),
        [like(code_weight), like(code_moments)],
        (sc, fix, spread, code_weight, code_moments, *early[:-1]),
        scalars=2,
    )
    logit_row = logit_bias.reshape(1, -1)
    bias_w, bias_m = in_biases.transpose(1, 0, 2), bias_moments.transpose(0, 2, 1, 3)
    vec_m, table_m = vector_moments.transpose(1, 0, 2), table_moments.transpose(1, 0, 2)
    bias_master, bias_state, vec_master, vec_state, table_master, table_state, logit_master, logit_state, loss_value, grad_norm = call(
        adam_small_kernel,
        [like(a) for a in (bias_w, bias_m, vectors, vec_m, rel_table, table_m, logit_row, logit_moments)]
        + [sds((1,), F32)] * 2,
        (sc, fix, spread, small, bias_w, bias_m, vectors, vec_m, rel_table, table_m, logit_row, logit_moments),
        scalars=2,
        scalar_outs=2,
    )
    return (
        loss_value, grad_norm,
        in_master.transpose(0, 2, 1, 3), in_state.transpose(0, 1, 3, 2, 4),
        out_master, out_state, patch_master, patch_state, code_master, code_state,
        bias_master.transpose(1, 0, 2), bias_state.transpose(0, 2, 1, 3),
        vec_master, vec_state.transpose(1, 0, 2), table_master, table_state.transpose(1, 0, 2),
        logit_master.reshape(-1), logit_state,
    )


def solution(mesh):
    in_specs = (
        P("dp", None, None),
        P("dp", None),
        P(),
        P("dp", None),
        P(),
        P(None, "dp", None, "tensor"),
        P(None, None, "dp", None, "tensor"),
        P(None, None, "tensor", "dp"),
        P(None, None, None, "tensor", "dp"),
        P("dp", None),
        P(None, "dp", None),
        P("dp", "tensor"),
        P(None, "dp", "tensor"),
        P(None, None, "tensor"),
        P(None, None, None, "tensor"),
        P(),
        P(),
        P("tensor", None),
        P(None, "tensor", None),
        P("tensor"),
        P(None, "tensor"),
    )
    out_specs = (P(), P()) + in_specs[5:]

    return jax.shard_map(local, mesh=mesh, in_specs=in_specs, out_specs=out_specs, check_vma=False)
```

```python
import functools

import jax
import jax.numpy as jnp
from jax import lax
from jax.experimental import pallas as pl
from jax.experimental.pallas import tpu as pltpu
from jax.sharding import PartitionSpec as P


HD = 64
GRID = 14
SPAN = 27
NPATCH = 196
ROWS = 208
NREL = 732
WIDE = 768

EPS_NORM = 1e-06
CLIP_NORM = 3.0
LEARN_RATE = 0.1
BETA_ONE = 0.9
BETA_TWO = 0.999
ADAM_EPS = 1e-08
WEIGHT_DECAY = 0.05
MASKED = -1e30

BF = jnp.bfloat16
F32 = jnp.float32


CODE_GROUPS = (10, 6)
CODE_PIECES = (5, 11)


S_DP, S_TP, S_CORE, S_X, S_Z, S_COUNT0, S_COUNT1, S_TOTAL = range(8)


def dot_nn(left, right):
    return lax.dot_general(left, right, (((1,), (0,)), ((), ())), preferred_element_type=F32)


def dot_nt(left, right):
    return lax.dot_general(left, right, (((1,), (1,)), ((), ())), preferred_element_type=F32)


def dot_tn(left, right):
    return lax.dot_general(left, right, (((0,), (0,)), ((), ())), preferred_element_type=F32)


def norm_parts(rows):
    average = jnp.mean(rows, axis=-1, keepdims=True)
    centred = rows - average
    inverse = lax.rsqrt(jnp.mean(centred * centred, axis=-1, keepdims=True) + EPS_NORM)
    return centred * inverse, inverse


def norm_back(upstream, gain, unit, inverse):
    scaled = upstream * gain
    return inverse * (
        scaled
        - jnp.mean(scaled, axis=-1, keepdims=True)
        - unit * jnp.mean(scaled * unit, axis=-1, keepdims=True)
    )


def column_sum(rows):
    return jnp.sum(rows, axis=0, keepdims=True)


def call(kernel, outs, args, scratch=(), flops=0, scalars=1, scalar_outs=0):
    moved = sum(a.size * a.dtype.itemsize for a in args) + sum(
        o.size * o.dtype.itemsize for o in outs
    )
    return pl.pallas_call(
        kernel,
        out_shape=tuple(outs),
        in_specs=[pl.BlockSpec(memory_space=pltpu.SMEM)] * scalars
        + [pl.BlockSpec(memory_space=pltpu.VMEM)] * (len(args) - scalars),
        out_specs=(pl.BlockSpec(memory_space=pltpu.VMEM),) * (len(outs) - scalar_outs)
        + (pl.BlockSpec(memory_space=pltpu.SMEM),) * scalar_outs,
        scratch_shapes=list(scratch),
        compiler_params=pltpu.CompilerParams(vmem_limit_bytes=60 * 1024 * 1024),
        cost_estimate=pl.CostEstimate(flops=flops, bytes_accessed=moved, transcendentals=0),
    )(*args)


def sds(shape, dtype):
    return jax.ShapeDtypeStruct(shape, dtype)


def dp_permute(value, bits, count):
    return lax.ppermute(value, "dp", [(i, i ^ bits) for i in range(count)])


def tp_permute(value, bits):
    return lax.ppermute(value, "tensor", [(i, i ^ bits) for i in range(4)])


def gather_blocks(block):
    count = lax.axis_size("dp")
    if count != 8:
        whole = lax.all_gather(block, "dp", axis=1, tiled=True)
        return [whole]
    along_z = [dp_permute(block, 2 * k, count) for k in (1, 2, 3)]
    across = dp_permute(block, 1, count)
    rest = [dp_permute(part, 1, count) for part in along_z]
    return [block, across, along_z[0], rest[0], along_z[1], rest[1], along_z[2], rest[2]]


def weight_scratch(blocks):
    pages, rows, wide = blocks[0].shape
    return pltpu.VMEM((pages, len(blocks), rows, wide), blocks[0].dtype)


def assemble(sc, block_refs, scratch):
    count = len(block_refs)
    own = sc[S_DP]
    for k, ref in enumerate(block_refs):
        place = lax.bitwise_xor(own, k) if count > 1 else 0
        scratch[:, place] = ref[...]
    _, _, rows, wide = scratch.shape
    return lambda page: scratch[page].reshape(count * rows, wide)


def emit(sc, page, value, outs, scratch):
    value = value.astype(BF)
    if len(outs) == 1:
        outs[0][page] = value
        return
    keep, give = outs
    scratch[...] = value.reshape(scratch.shape)
    x = sc[S_X]
    for z in range(4):
        keep[page, z] = scratch[2 * z + x]
        give[page, z] = scratch[2 * z + 1 - x]


def grad_outs(pages, rows, wide, count):
    if count != 8:
        return [sds((pages, rows, wide), BF)]
    return [sds((pages, 4, rows // 8, wide), BF)] * 2


def grad_scratch(rows, wide):
    return pltpu.VMEM((8, rows // 8, wide), BF)


def sum_x_kernel(sc, keep, got, own, one, two, three, total):
    total[...] = keep[...].astype(F32) + got[...].astype(F32)
    z = sc[S_Z]
    own[...] = total[:, z]
    one[...] = total[:, lax.bitwise_xor(z, 1)].astype(BF)
    two[...] = total[:, lax.bitwise_xor(z, 2)].astype(BF)
    three[...] = total[:, lax.bitwise_xor(z, 3)].astype(BF)


def add_parts(parts):
    values = [part[...].astype(F32) for part in parts]
    if len(values) < 4:
        return values[0] if len(values) == 1 else values[0] + values[1]
    return (values[0] + values[1]) + (values[2] + values[3])


def square_sum(value):
    while value.ndim > 2:
        value = value.reshape((-1,) + value.shape[-1:]) if value.ndim == 3 else value[0]
    rows = jnp.sum(value * value, axis=0, keepdims=True)
    return jnp.sum(rows, axis=1, keepdims=True)


def sum_early_kernel(counts, sc, *refs):
    squares, at, total = refs[-1], sum(counts), jnp.zeros((1, 1), F32)
    first = 0
    for g, count in enumerate(counts):
        value = add_parts(refs[first : first + count])
        first += count
        refs[at + g][...] = value
        total += square_sum(value)
    squares[...] = jnp.broadcast_to(total, (8, 128))


def late_rows(ref):
    half = WIDE // 4
    rows = (ref.shape[0] * 2) // 5
    pages = ref[0 : 2 * rows, :].astype(F32).reshape(2, rows, ref.shape[1])
    patch = jnp.concatenate([ref[2 * rows :, 0:half], ref[2 * rows :, half:]], axis=0).astype(F32)
    return pages, patch


def sum_x_late_kernel(sc, keep, got, keep_patch, got_patch, own, own_patch, one, two, three, total, total_patch):
    total[...] = keep[...].astype(F32) + got[...].astype(F32)
    total_patch[...] = keep_patch[0].astype(F32) + got_patch[0].astype(F32)
    z = sc[S_Z]
    own[...] = total[:, z]
    own_patch[0] = total_patch[z]
    rows, half = own.shape[1], own_patch.shape[2]
    for k, ref in enumerate((one, two, three)):
        to = lax.bitwise_xor(z, k + 1)
        for page in range(2):
            ref[rows * page : rows * (page + 1), :] = total[page, to].astype(BF)
        for page in range(2):
            piece = total_patch[to, rows // 2 * page : rows // 2 * (page + 1), :]
            ref[2 * rows :, half * page : half * (page + 1)] = piece.astype(BF)


def sum_late_kernel(travelled, small_parts, dp, tp, sc, early, own, own_patch, *refs):
    blocks, parts = refs[:travelled], refs[travelled : travelled + small_parts]
    shard, patch_shard, small, shares = refs[travelled + small_parts :]
    value, patch = own[...], own_patch[0]
    if travelled:
        (one, p1), (two, p2), (three, p3) = [late_rows(ref) for ref in blocks]
        value = (value + one) + (two + three)
        patch = (patch + p1) + (p2 + p3)
    shard[...] = value
    patch_shard[0] = patch
    held = add_parts(parts)
    small[...] = held
    row = lax.broadcasted_iota(jnp.int32, (held.shape[0], 1), 0)
    weight = jnp.where(row < 13, (1.0 / (dp * tp)) ** 0.5, (1.0 / dp) ** 0.5)
    held = held * jnp.where(row < held.shape[0] - 1, weight, 0.0)
    total = early[0:1, 0:1] + square_sum(value) + square_sum(patch) + square_sum(held)
    shares[...] = jnp.broadcast_to(total.reshape(1, 1, 1), shares.shape)


def z_first_kernel(first, wide, sc, picked, grad, own, one, two, three, scratch):
    scratch[...] = dot_tn(picked[...], grad[:, first : first + wide]).astype(BF).reshape(scratch.shape)
    for k, ref in enumerate((own, one, two, three)):
        to = lax.bitwise_xor(sc[S_Z], k)
        for x in range(2):
            ref[x] = scratch[2 * to + x]


def sum_z_first_kernel(sc, own, one, two, three, kept, sent, total):
    total[...] = add_parts((own, one, two, three))
    x = sc[S_X]
    kept[0] = total[x]
    sent[0] = total[1 - x].astype(BF)


def z_first_start(sc, parts):
    own, *sends = parts
    count = lax.axis_size("dp")
    got = [dp_permute(part, 2 * k + 2, count) for k, part in enumerate(sends)]
    _, rows, wide = own.shape
    kept, sent = call(
        sum_z_first_kernel,
        [sds((1, rows, wide), F32), sds((1, rows, wide), BF)],
        (sc, own, *got),
        [pltpu.VMEM(own.shape, F32)],
    )
    return [kept, dp_permute(sent, 1, count)]


def scatter_start(sc, grads):
    count = lax.axis_size("dp")
    if count != 8:
        return [lax.psum_scatter(grads[0].astype(F32), "dp", scatter_dimension=1, tiled=True)]
    keep, give = grads
    got = dp_permute(give, 1, count)
    pages, _, rows, wide = keep.shape
    block = (pages, rows, wide)
    own, one, two, three = call(
        sum_x_kernel, [sds(block, F32)] + [sds(block, BF)] * 3, (sc, keep, got), [pltpu.VMEM(keep.shape, F32)]
    )
    one = dp_permute(one, 2, count)
    two = dp_permute(two, 4, count)
    three = dp_permute(three, 6, count)
    return [own, one, two, three]


def sum_early(sc, started):
    outs = call(
        functools.partial(sum_early_kernel, [len(s) for s in started]),
        [sds(s[0].shape, F32) for s in started] + [sds((8, 128), F32)],
        (sc, *[part for s in started for part in s]),
    )
    return list(outs[:-1]), outs[-1]


def late_start(sc, grads, patch_grads):
    count = lax.axis_size("dp")
    if count != 8:
        return scatter_start(sc, grads) + scatter_start(sc, patch_grads)
    keep, give = grads
    keep_patch, give_patch = patch_grads
    got = dp_permute(give, 1, count)
    got_patch = dp_permute(give_patch, 1, count)
    pages, _, rows, wide = keep.shape
    half = keep_patch.shape[3]
    own, own_patch, *blocks = call(
        sum_x_late_kernel,
        [sds((pages, rows, wide), F32), sds((1, rows, half), F32)] + [sds((5 * rows // 2, wide), BF)] * 3,
        (sc, keep, got, keep_patch, got_patch),
        [pltpu.VMEM(keep.shape, F32), pltpu.VMEM(keep_patch.shape[1:], F32)],
    )
    return [own, own_patch] + [dp_permute(b, 2 * k + 2, count) for k, b in enumerate(blocks)]


def sum_late(sc, early, started, small_parts, dp, tp):
    return call(
        functools.partial(sum_late_kernel, len(started) - 2, len(small_parts), dp, tp),
        [sds(a.shape, F32) for a in (started[0], started[1], small_parts[0])] + [sds((dp * tp, 8, 128), F32)],
        (sc, early, *started, *small_parts),
    )


def small_start(value):
    count = lax.axis_size("dp")
    if count != 8:
        return [lax.psum(value, "dp")]
    value = value + dp_permute(value, 1, count)
    return [value] + [dp_permute(value, 2 * k, count) for k in (1, 2, 3)]


def tensor_gather(value):
    across = tp_permute(value, 2)
    return [value, tp_permute(value, 1), across, tp_permute(across, 1)]


def tensor_sum(keep, send):
    pair = (keep.astype(F32) + tp_permute(send, 1).astype(F32)).astype(BF)
    own = (pair.astype(F32) + tp_permute(pair, 2).astype(F32)).astype(BF)
    return own, tp_permute(own, 1)


def split_dot(dot, left, right, parts):
    total = None
    for _ in range(parts):
        part = right.astype(BF)
        right = right - part.astype(F32)
        value = dot(left, part)
        total = value if total is None else total + value
    return total


def spread_matrix(dtype):
    j = lax.broadcasted_iota(jnp.int32, (ROWS, 384), 0)
    k = lax.broadcasted_iota(jnp.int32, (ROWS, 384), 1)
    tall = lax.shift_right_logical(j * 4682, 16)
    place = SPAN * (GRID - 1 - tall) + (GRID - 1) - (j - GRID * tall)
    return jnp.where((place == k) & (j < NPATCH), 1.0, 0.0).astype(dtype)


def table_kernel(sc, table, bias, stage):
    spread = spread_matrix(BF)
    row16 = lax.broadcasted_iota(jnp.int32, (16, WIDE), 0)
    i = lax.broadcasted_iota(jnp.int32, (ROWS, ROWS), 0)
    j = lax.broadcasted_iota(jnp.int32, (ROWS, ROWS), 1)

    @pl.loop(0, table.shape[0])
    def _(h):
        held = table[pl.ds(h, 1), :]
        line = jnp.concatenate([held, jnp.zeros((1, WIDE - NREL), F32)], axis=1)
        wide = jnp.broadcast_to(line, (16, WIDE))
        shifted = wide
        for c in range(1, GRID):
            shifted = jnp.where(row16 == c, pltpu.roll(wide, WIDE - c, 1), shifted)
        stage[...] = jnp.zeros(stage.shape, F32)
        for r in range(GRID):
            turned = shifted if r == 0 else pltpu.roll(shifted, WIDE - SPAN * r, 1)
            stage[GRID * r : GRID * r + 16, :] = turned[:, 0:384]
        inner = split_dot(lambda one, two: dot_nt(two, one), spread, stage[...], 3)
        to_all = held[:, NREL - 3 : NREL - 2]
        to_class = held[:, NREL - 2 : NREL - 1]
        corner = held[:, NREL - 1 : NREL]
        edge = jnp.where(j == NPATCH, corner, to_all)
        inner = jnp.where(i == NPATCH, edge, jnp.where(j == NPATCH, to_class, inner))
        inner = jnp.where(i > NPATCH, 0.0, inner)
        bias[h] = jnp.where(j > NPATCH, MASKED, inner)


def covered_rows(sc, places, image):
    slots = places.shape[1]
    patch = lax.broadcasted_iota(jnp.int32, (NPATCH, slots), 0)
    slot = lax.broadcasted_iota(jnp.int32, (NPATCH, slots), 1)
    hit = (patch == places[pl.ds(image, 1), :]) & (slot < sc[S_COUNT0 + image])
    return jnp.max(jnp.where(hit, 1.0, 0.0), axis=1, keepdims=True)


def picks(places, image, slots):
    row = lax.broadcasted_iota(jnp.int32, (slots, ROWS), 1)
    return row == places[image * slots : (image + 1) * slots, :]


def rows_of(image):
    return pl.ds(pl.multiple_of(image * ROWS, 16), ROWS)


def heads_of(array, image, h, first=0):
    return array[rows_of(image), first + HD * h : first + HD * (h + 1)]


def order_quarters(sc, quarters, scratch):
    for k, ref in enumerate(quarters):
        scratch[lax.bitwise_xor(sc[S_TP], k)] = ref[...]


def patch_kernel(blocks, sc, *refs):
    page = assemble(sc, refs[:blocks], refs[-1])
    refs[blocks][...] = page(0)


def attend_kernel(blocks, sc, images, places, vectors, biases, bias, *refs):
    quarters, weight_refs = refs[:4], refs[4 : 4 + blocks]
    stream_ref, qk_ref, v_ref, heads_ref, entered_ref, keep, send, weights, term, patch = refs[4 + blocks :]
    share = v_ref.shape[1]
    page = assemble(sc, weight_refs, weights)
    order_quarters(sc, quarters, patch)
    final = vectors.shape[0] - 5

    @pl.loop(0, 2)
    def _(b):
        held = images[b]
        covered = covered_rows(sc, places, b)
        embedded = jnp.concatenate([dot_nn(held, patch[k]) for k in range(4)], axis=1)
        embedded = embedded + vectors[final + 2 : final + 3, :]
        embedded = embedded * (1.0 - covered) + vectors[final + 4 : final + 5, :] * covered
        stream_ref[b, 192:ROWS, :] = jnp.zeros((ROWS - 192, WIDE), F32)
        stream_ref[b, 0:NPATCH, :] = embedded
        stream_ref[b, NPATCH : NPATCH + 1, :] = vectors[final + 3 : final + 4, :]

    unit, _ = norm_parts(stream_ref[...].reshape(2 * ROWS, WIDE))
    entered = (unit * vectors[0:1, :] + vectors[1:2, :]).astype(BF)
    entered_ref[...] = entered
    joined = dot_nn(entered, page(0))
    shift = jnp.concatenate([biases[0, 0:1, :], jnp.zeros((1, share), F32)], axis=1)
    qk_ref[...] = (joined + shift).astype(BF)
    second = page(1)
    v_ref[...] = (dot_nn(entered, second[:, 0:share]) + biases[0, 1:2, :]).astype(BF)

    @pl.loop(0, 2)
    def _(b):
        for h in range(share // HD):
            scores = dot_nt(heads_of(qk_ref, b, h), heads_of(qk_ref, b, h, share)) * 0.125 + bias[h]
            scores = jnp.exp(scores - jnp.max(scores, axis=1, keepdims=True))
            soft = scores / jnp.sum(scores, axis=1, keepdims=True)
            heads_ref[rows_of(b), HD * h : HD * (h + 1)] = dot_nn(soft.astype(BF), heads_of(v_ref, b, h)).astype(BF)

    term[...] = dot_nt(heads_ref[...], second[:, share:]).astype(BF).reshape(term.shape)
    keep[...] = term[sc[S_CORE]]
    send[...] = term[1 - sc[S_CORE]]


def add_branch(sc, out, base, own, other, gamma, shift):
    core = sc[S_CORE]
    out[core] = base[core] + gamma * (own[...].astype(F32) + shift)
    out[1 - core] = base[1 - core] + gamma * (other[...].astype(F32) + shift)


def feed_kernel(blocks, sc, stream, own, other, vectors, biases, *refs):
    weight_refs = refs[:blocks]
    middle, pre_ref, active_ref, entered_ref, keep, send, weights, term = refs[blocks:]
    page = assemble(sc, weight_refs, weights)
    add_branch(sc, middle, stream, own, other, vectors[3:4, :], vectors[2:3, :])
    unit, _ = norm_parts(middle[...].reshape(2 * ROWS, WIDE))
    entered = (unit * vectors[4:5, :] + vectors[5:6, :]).astype(BF)
    entered_ref[...] = entered
    total = None
    half = WIDE // 2
    for g in range(2):
        shift = jnp.concatenate([biases[0, 2 + 2 * g : 3 + 2 * g, :], biases[0, 3 + 2 * g : 4 + 2 * g, :]], axis=1)
        pre = dot_nn(entered, page(g)) + shift
        pre_ref[:, half * g : half * (g + 1)] = pre
        active = (0.5 * pre * (1.0 + lax.erf(pre * 0.7071067811865476))).astype(BF)
        active_ref[:, half * g : half * (g + 1)] = active
        part = dot_nt(active, page(2 + g))
        total = part if total is None else total + part
    term[...] = total.astype(BF).reshape(term.shape)
    keep[...] = term[sc[S_CORE]]
    send[...] = term[1 - sc[S_CORE]]


def logit_kernel(blocks, sc, middle, own, other, vectors, places, codes, logit_bias, *refs):
    stream, picked_ref, logits_ref, stats, weights, more_weights = refs[2 * blocks :]
    pages = (assemble(sc, refs[:blocks], weights)(0), assemble(sc, refs[blocks : 2 * blocks], more_weights)(0))
    final = vectors.shape[0] - 5
    slots = places.shape[0] // 2
    add_branch(sc, stream, middle, own, other, vectors[7:8, :], vectors[6:7, :])
    wanted = []
    for b in range(2):
        unit, _ = norm_parts(stream[b])
        closing = (unit * vectors[final : final + 1, :] + vectors[final + 1 : final + 2, :]).astype(BF)
        hit = picks(places, b, slots)
        picked_ref[b * slots : (b + 1) * slots, :] = dot_nn(jnp.where(hit, 1.0, 0.0).astype(BF), closing).astype(BF)
        found = jnp.where(hit[:, 0:NPATCH], codes[b : b + 1, :].astype(F32), 0.0)
        wanted.append(jnp.sum(found, axis=1, keepdims=True))
    wanted = jnp.concatenate(wanted, axis=0)
    first = 0
    for page in pages:
        last = first + page.shape[1]
        logits_ref[:, first:last] = dot_nn(picked_ref[...], page) + logit_bias[:, first:last]
        first = last
    logits = logits_ref[...]
    share = logits.shape[1]
    first = (sc[S_TP] * share).astype(F32)
    column = lax.broadcasted_iota(jnp.int32, logits.shape, 1).astype(F32)
    peak = jnp.max(logits, axis=1, keepdims=True)
    summed = jnp.sum(jnp.exp(logits - peak), axis=1, keepdims=True)
    chosen = jnp.sum(jnp.where(column == wanted - first, logits, 0.0), axis=1, keepdims=True)
    lane = lax.broadcasted_iota(jnp.int32, stats.shape, 1)
    stats[...] = jnp.where(lane == 0, peak, jnp.where(lane == 1, summed, jnp.where(lane == 2, chosen, wanted)))


def join_stats(one, two):
    peak = jnp.maximum(one[0], two[0])
    summed = one[1] * jnp.exp(one[0] - peak) + two[1] * jnp.exp(two[0] - peak)
    return peak, summed, one[2] + two[2]


def loss_kernel(blocks, sc, own, one, two, three, logits_ref, *refs):
    grad_ref, shift_ref, loss_ref, keep, send, weights, more_weights, term = refs[2 * blocks :]
    pages = (assemble(sc, refs[:blocks], weights)(0), assemble(sc, refs[blocks : 2 * blocks], more_weights)(0))
    logits = logits_ref[...]
    slots = logits.shape[0] // 2
    share = logits.shape[1]
    held = [tuple(ref[:, k : k + 1] for k in range(3)) for ref in (own, one, two, three)]
    peak, summed, chosen = join_stats(join_stats(held[0], held[1]), join_stats(held[2], held[3]))
    logsum = peak + jnp.log(summed)
    slot = lax.broadcasted_iota(jnp.int32, (2 * slots, 1), 0)
    live = jnp.where(
        slot < slots,
        jnp.where(slot < sc[S_COUNT0], 1.0, 0.0),
        jnp.where(slot - slots < sc[S_COUNT1], 1.0, 0.0),
    )
    total = jnp.full((2 * slots, 1), sc[S_TOTAL], jnp.int32).astype(F32)
    loss_ref[...] = jnp.broadcast_to(column_sum(live * (logsum - chosen)), loss_ref.shape)
    first = (sc[S_TP] * share).astype(F32)
    column = lax.broadcasted_iota(jnp.int32, logits.shape, 1).astype(F32)
    matched = jnp.where(column == own[:, 3:4] - first, 1.0, 0.0)
    grad = ((live / total) * (jnp.exp(logits - logsum) - matched)).astype(BF)
    grad_ref[...] = grad
    shift_ref[...] = column_sum(grad.astype(F32))
    wide = pages[0].shape[1]
    total = dot_nt(grad[:, :wide], pages[0]) + dot_nt(grad[:, wide:], pages[1])
    term[...] = total.astype(BF).reshape(term.shape)
    keep[...] = term[sc[S_CORE]]
    send[...] = term[1 - sc[S_CORE]]


def code_grad_kernel(first, wide, sc, picked, grad, *refs):
    outs, scratch = refs[:-1], refs[-1]
    emit(sc, 0, dot_tn(picked[...], grad[:, first : first + wide]), outs, scratch)


def branch_back(sc, gated_ref, sums, first, upstream, own, other, gamma, shift):
    core = sc[S_CORE]
    gamma_sum = column_sum(upstream[core] * (own[...].astype(F32) + shift)) + column_sum(
        upstream[1 - core] * (other[...].astype(F32) + shift)
    )
    sums[first + 1 : first + 2, :] = gamma_sum
    gated = upstream[...].reshape(2 * ROWS, WIDE) * gamma
    sums[first : first + 1, :] = column_sum(gated)
    gated_ref[...] = gated.astype(BF)


def feed_back_kernel(blocks, sc, own, other, places, stream, branch_own, branch_other, vectors, pre_ref, *refs):
    weight_refs = refs[:blocks]
    upstream, gated_ref, grad_pre_ref, sums, keep, send, weights, term, picked = refs[blocks:]
    page = assemble(sc, weight_refs, weights)
    core = sc[S_CORE]
    final = vectors.shape[0] - 5
    slots = places.shape[0] // 2
    picked[core] = own[...]
    picked[1 - core] = other[...]
    gain_sum = jnp.zeros((1, WIDE), F32)
    shift_sum = jnp.zeros((1, WIDE), F32)
    for b in range(2):
        hit = jnp.where(picks(places, b, slots), 1.0, 0.0).astype(BF)
        closing = dot_tn(hit, picked[b])
        unit, inverse = norm_parts(stream[b])
        gain_sum += column_sum(closing * unit)
        shift_sum += column_sum(closing)
        upstream[b] = norm_back(closing, vectors[final : final + 1, :], unit, inverse)
    sums[0:1, :] = gain_sum
    sums[1:2, :] = shift_sum
    branch_back(sc, gated_ref, sums, 2, upstream, branch_own, branch_other, vectors[7:8, :], vectors[6:7, :])
    gated = gated_ref[...]
    total = None
    half = WIDE // 2
    for g in range(2):
        pre = pre_ref[:, half * g : half * (g + 1)]
        grad_active = dot_nn(gated, page(2 + g))
        slope = 0.5 * (1.0 + lax.erf(pre * 0.7071067811865476)) + pre * (
            jnp.exp(-0.5 * pre * pre) * 0.3989422804014327
        )
        grad_pre = (grad_active * slope).astype(BF)
        grad_pre_ref[:, half * g : half * (g + 1)] = grad_pre
        sums[4:5, half * g : half * (g + 1)] = column_sum(grad_pre.astype(F32))
        part = dot_nt(grad_pre, page(g))
        total = part if total is None else total + part
    term[...] = total.astype(BF).reshape(term.shape)
    keep[...] = term[core]
    send[...] = term[1 - core]


def feed_grad_kernel(sc, entered, grad_pre, gated, active, *refs):
    outs, scratch = refs[:-1], refs[-1]
    half = WIDE // 2

    @pl.loop(0, 2)
    def _(g):
        columns = pl.ds(pl.multiple_of(half * g, 128), half)
        emit(sc, g, dot_tn(entered[...], grad_pre[:, columns]), outs, scratch)
        emit(sc, 2 + g, dot_tn(gated[...], active[:, columns]), outs, scratch)


def attend_back_kernel(
    blocks, sc, own, other, upstream, middle, branch_own, branch_other, vectors, qk, v, bias, *refs
):
    weight_refs = refs[:blocks]
    passed, gated_ref, grad_qk, grad_v, sums, table_sums, keep, send = refs[blocks : blocks + 8]
    weights, term, grad_heads, stage, together = refs[blocks + 8 :]
    page = assemble(sc, weight_refs, weights)
    core = sc[S_CORE]
    share = v.shape[1]
    gain = vectors[4:5, :]
    gain_sum = jnp.zeros((1, WIDE), F32)
    shift_sum = jnp.zeros((1, WIDE), F32)
    for image, arrived in ((core, own), (1 - core, other)):
        grad = arrived[...].astype(F32)
        unit, inverse = norm_parts(middle[image])
        gain_sum += column_sum(grad * unit)
        shift_sum += column_sum(grad)
        passed[image] = upstream[image] + norm_back(grad, gain, unit, inverse)
    sums[0:1, :] = gain_sum
    sums[1:2, :] = shift_sum
    branch_back(sc, gated_ref, sums, 2, passed, branch_own, branch_other, vectors[3:4, :], vectors[2:3, :])
    second = page(1)
    grad_heads[...] = dot_nn(gated_ref[...], second[:, share:]).astype(BF)
    spread = spread_matrix(BF)
    lane = lax.broadcasted_iota(jnp.int32, (1, WIDE), 1)
    row16 = lax.broadcasted_iota(jnp.int32, (16, WIDE), 0)
    i = lax.broadcasted_iota(jnp.int32, (ROWS, ROWS), 0)
    j = lax.broadcasted_iota(jnp.int32, (ROWS, ROWS), 1)

    for b in range(2):
        rows = rows_of(b)
        for h in range(share // HD):
            queries, keys, values = heads_of(qk, b, h), heads_of(qk, b, h, share), heads_of(v, b, h)
            scores = dot_nt(queries, keys) * 0.125 + bias[h]
            scores = jnp.exp(scores - jnp.max(scores, axis=1, keepdims=True))
            soft = scores / jnp.sum(scores, axis=1, keepdims=True)
            grad_out = heads_of(grad_heads, b, h)
            grad_v[rows, HD * h : HD * (h + 1)] = dot_tn(soft.astype(BF), grad_out).astype(BF)
            grad_soft = dot_nt(grad_out, values)
            grad_scores = soft * (grad_soft - jnp.sum(soft * grad_soft, axis=1, keepdims=True))
            grad_scores = grad_scores.astype(BF)
            grad_qk[rows, HD * h : HD * (h + 1)] = (dot_nn(grad_scores, keys) * 0.125).astype(BF)
            grad_qk[rows, share + HD * h : share + HD * (h + 1)] = (dot_tn(grad_scores, queries) * 0.125).astype(BF)
            together[b, h] = grad_scores

    for h in range(share // HD):
        stage[...] = dot_nn(together[0, h], spread) + dot_nn(together[1, h], spread)
        lined = jnp.zeros((16, WIDE), F32)
        for r in range(GRID):
            piece = jnp.concatenate([stage[GRID * r : GRID * r + 16, :], jnp.zeros((16, WIDE - 384), F32)], axis=1)
            lined += piece if r == 0 else pltpu.roll(piece, SPAN * r, 1)
        folded = jnp.where(row16 == 0, lined, 0.0)
        for c in range(1, GRID):
            folded += pltpu.roll(jnp.where(row16 == c, lined, 0.0), c, 1)
        line = column_sum(folded)
        on_row, on_column = i == NPATCH, j == NPATCH
        added = together[0, h].astype(F32) + together[1, h].astype(F32)
        to_all = jnp.sum(jnp.where(on_row & (j < NPATCH), added, 0.0))
        to_class = jnp.sum(jnp.where(on_column & (i < NPATCH), added, 0.0))
        corner = jnp.sum(jnp.where(on_row & on_column, added, 0.0))
        line = jnp.where(lane == NREL - 3, to_all, line)
        line = jnp.where(lane == NREL - 2, to_class, line)
        line = jnp.where(lane == NREL - 1, corner, line)
        table_sums[pl.ds(h, 1), :] = line

    sums[4:5, 0:share] = column_sum(grad_qk[:, 0:share].astype(F32))
    sums[4:5, share : 2 * share] = column_sum(grad_v[...].astype(F32))
    sums[4:5, 2 * share :] = jnp.zeros((1, WIDE - 2 * share), F32)
    total = dot_nt(grad_qk[...], page(0)) + dot_nt(grad_v[...], second[:, 0:share])
    term[...] = total.astype(BF).reshape(term.shape)
    keep[...] = term[core]
    send[...] = term[1 - core]


def attend_grad_kernel(sc, entered_ref, grad_qk, grad_v, gated, heads, *refs):
    outs, scratch = refs[:-1], refs[-1]
    entered = entered_ref[...]
    emit(sc, 0, dot_tn(entered, grad_qk[...]), outs, scratch)
    pair = jnp.concatenate([dot_tn(entered, grad_v[...]), dot_tn(gated[...], heads[...])], axis=1)
    emit(sc, 1, pair, outs, scratch)


def embed_back_kernel(sc, own, other, passed, stream, vectors, images, places, feed_sums, attend_sums, table_sums, logit_sums, loss, *refs):
    small, outs = refs[0], refs[1:-3]
    scratch, grads, quarters = refs[-3:]
    core = sc[S_CORE]
    gain = vectors[0:1, :]
    zero = jnp.zeros((1, WIDE), F32)
    gain_sum, shift_sum = zero, zero
    for image, arrived in ((core, own), (1 - core, other)):
        grad = arrived[...].astype(F32)
        unit, inverse = norm_parts(stream[image])
        gain_sum += column_sum(grad * unit)
        shift_sum += column_sum(grad)
        grads[image] = passed[image] + norm_back(grad, gain, unit, inverse)
    patch_sum, class_sum, mask_sum = zero, zero, zero
    quarter = WIDE // 4
    for b in range(2):
        grad = grads[b, 0:NPATCH, :]
        covered = covered_rows(sc, places, b)
        through = grad * (1.0 - covered)
        patch_sum += column_sum(through)
        mask_sum += column_sum(grad * covered)
        class_sum += grads[b, NPATCH : NPATCH + 1, :]
        through = through.astype(BF)
        for k in range(4):
            quarters[k, b] = through[:, quarter * k : quarter * (k + 1)]
    mine = sc[S_TP]
    emit(sc, 0, dot_tn(images[0], quarters[mine, 0]) + dot_tn(images[1], quarters[mine, 1]), outs, scratch)
    small[...] = jnp.zeros(small.shape, F32)
    small[0:1, :] = gain_sum
    small[1:2, :] = shift_sum
    small[2:4, :] = attend_sums[2:4, :]
    small[4:6, :] = attend_sums[0:2, :]
    small[6:8, :] = feed_sums[2:4, :]
    small[8:10, :] = feed_sums[0:2, :]
    small[10:11, :] = patch_sum
    small[11:12, :] = class_sum
    small[12:13, :] = mask_sum
    small[13:14, :] = attend_sums[4:5, :]
    small[14:15, :] = feed_sums[4:5, :]
    heads = table_sums.shape[0]
    small[15 : 15 + heads, :] = table_sums[...]
    first = 15 + heads
    left = logit_sums.shape[1]
    row = 0
    while left > 0:
        take = min(left, WIDE)
        small[first + row : first + row + 1, 0:take] = logit_sums[:, row * WIDE : row * WIDE + take]
        left -= take
        row += 1
    small[first + row : first + row + 1, 0:128] = loss[...]


def clip_of(spread):
    norm = jnp.sqrt(jnp.sum(spread[...], axis=0)[0:1, 0:1])
    return norm, jnp.minimum(1.0, CLIP_NORM / (norm + 1e-06))


def adam(master, first_old, root_old, gradient, fix, decay):
    clip, first_fix, second_fix = fix
    clipped = gradient * clip
    first = BETA_ONE * first_old + (1.0 - BETA_ONE) * clipped
    root = jnp.sqrt(BETA_TWO * root_old * root_old + (1.0 - BETA_TWO) * clipped * clipped)
    direction = first / first_fix / (root / second_fix + ADAM_EPS) + decay * master
    return master - LEARN_RATE * direction, first, root


def adam_matrix_kernel(
    sc, fix_ref, spread, in_w, in_m, out_w, out_m, patch_w, patch_m, first, feed, patch0, patch1, patch2, patch3,
    in_master, in_state, out_master, out_state, patch_master, patch_state, patch,
):
    fix = (clip_of(spread)[1], fix_ref[0], fix_ref[1])
    order_quarters(sc, (patch0, patch1, patch2, patch3), patch)
    share = in_w.shape[3]
    half = 2 * share

    def into(j, gradient):
        in_master[0, j], in_state[0, 0, j], in_state[1, 0, j] = adam(
            in_w[0, j], in_m[0, 0, j], in_m[1, 0, j], gradient, fix, WEIGHT_DECAY
        )

    def outof(j, gradient):
        out_master[0, j], out_state[0, 0, j], out_state[1, 0, j] = adam(
            out_w[0, j], out_m[0, 0, j], out_m[1, 0, j], gradient.T, fix, WEIGHT_DECAY
        )

    into(0, first[0, :, 0:share])
    into(1, first[0, :, share:half])
    into(2, first[1, :, 0:share])
    outof(0, first[1, :, share:half])

    @pl.loop(0, 2)
    def _(g):
        for k in range(2):
            into(3 + 2 * g + k, feed[g, :, share * k : share * (k + 1)])
            outof(1 + 2 * g + k, feed[2 + g, :, share * k : share * (k + 1)])

    for g in range(4):
        columns = slice(g * share, (g + 1) * share)
        patch_master[:, columns], patch_state[0, :, columns], patch_state[1, :, columns] = adam(
            patch_w[:, columns], patch_m[0, :, columns], patch_m[1, :, columns], patch[g, 0], fix, WEIGHT_DECAY
        )


def adam_code_kernel(pieces, sc, fix_ref, spread, code_w, code_m, *refs):
    fix = (clip_of(spread)[1], fix_ref[0], fix_ref[1])
    grads = refs[:pieces]
    code_master, code_state = refs[pieces:]
    rows = code_w.shape[0]
    step = 8 if rows % 8 == 0 else rows

    @pl.loop(0, rows // step)
    def _(block):
        at = pl.ds(pl.multiple_of(block * step, step), step)
        first = 0
        for grad in grads:
            columns = slice(first, first + grad.shape[2])
            first += grad.shape[2]
            code_master[at, columns], code_state[0, at, columns], code_state[1, at, columns] = adam(
                code_w[at, columns], code_m[0, at, columns], code_m[1, at, columns], grad[0, at, :], fix, WEIGHT_DECAY
            )


def adam_small_kernel(
    sc, fix_ref, spread, small, bias_w, bias_m, vec_w, vec_m, table_w, table_m, logit_w, logit_m,
    bias_master, bias_state, vec_master, vec_state, table_master, table_state, logit_master, logit_state, loss_out, norm_out,
):
    norm, clip = clip_of(spread)
    fix = (clip, fix_ref[0], fix_ref[1])
    norm_out[0] = jnp.sum(norm)
    loss = small[small.shape[0] - 1 : small.shape[0], 0:1] / jnp.full((1, 1), sc[S_TOTAL], jnp.int32).astype(F32)
    loss_out[0] = jnp.sum(loss)
    share = bias_w.shape[2]
    for j in range(6):
        row, k = (13, j) if j < 2 else (14, j - 2)
        gradient = small[row : row + 1, share * k : share * (k + 1)]
        bias_master[j], bias_state[0, j], bias_state[1, j] = adam(
            bias_w[j], bias_m[0, j], bias_m[1, j], gradient, fix, 0.0
        )
    vec_master[...], vec_state[:, 0, :], vec_state[:, 1, :] = adam(
        vec_w[...], vec_m[:, 0, :], vec_m[:, 1, :], small[0:13, :], fix, 0.0
    )
    heads = table_w.shape[0]
    table_master[...], table_state[:, 0, :], table_state[:, 1, :] = adam(
        table_w[...], table_m[:, 0, :], table_m[:, 1, :], small[15 : 15 + heads, 0:NREL], fix, 0.0
    )
    first = 15 + heads
    share = logit_w.shape[1]
    gradient = jnp.concatenate(
        [small[first + k : first + k + 1, 0 : min(WIDE, share - k * WIDE)] for k in range(-(-share // WIDE))], axis=1
    )
    logit_master[...], logit_state[0:1, :], logit_state[1:2, :] = adam(
        logit_w[...], logit_m[0:1, :], logit_m[1:2, :], gradient, fix, 0.0
    )


def local(
    images, mask_places, mask_counts, codes, step_count,
    in_weights, in_moments, out_weights, out_moments, patch_weight, patch_moments,
    code_weight, code_moments, in_biases, bias_moments, vectors, vector_moments,
    rel_table, table_moments, logit_bias, logit_moments,
):
    dp = lax.axis_size("dp")
    tp = lax.axis_size("tensor")
    dp_index = lax.axis_index("dp").astype(jnp.int32)
    tp_index = lax.axis_index("tensor").astype(jnp.int32)
    share = in_weights.shape[3]
    code_share = code_weight.shape[1]
    slots = mask_places.shape[1]
    heads = rel_table.shape[0]
    own_counts = lax.dynamic_slice_in_dim(mask_counts, dp_index * 2, 2)
    total_count = jnp.sum(mask_counts)
    sc = jnp.stack(
        [dp_index, tp_index, tp_index & 1, dp_index & 1, dp_index >> 1, own_counts[0], own_counts[1], total_count]
    )

    into = in_weights[0].astype(BF)
    outof = out_weights[0].astype(BF).transpose(0, 2, 1)
    quarter = WIDE // tp
    patch_group = lax.dynamic_slice_in_dim(patch_weight, tp_index * quarter, quarter, 1).astype(BF)[None]

    def pair(one, two):
        return jnp.concatenate([one, two], axis=-1)

    first_group = jnp.stack(
        [pair(into[:, 0], into[:, 1]), pair(into[:, 2], outof[0])]
    )
    second_group = jnp.stack(
        [pair(into[:, 3], into[:, 4]), pair(into[:, 5], into[:, 6]), pair(outof[1], outof[2]), pair(outof[3], outof[4])]
    )
    code_cut = CODE_GROUPS[0] * code_share // sum(CODE_GROUPS)
    patch_blocks = gather_blocks(patch_group)
    first_blocks = gather_blocks(first_group)
    second_blocks = gather_blocks(second_group)
    code_blocks = gather_blocks(code_weight[:, :code_cut].astype(BF)[None])
    more_blocks = gather_blocks(code_weight[:, code_cut:].astype(BF)[None])
    nb = len(first_blocks)
    (patch_own,) = call(
        functools.partial(patch_kernel, nb), [sds((WIDE, quarter), BF)], (sc, *patch_blocks),
        [weight_scratch(patch_blocks)],
    )
    patch_quarters = tensor_gather(patch_own)

    (bias,) = call(table_kernel, [sds((heads, ROWS, ROWS), F32)], (sc, rel_table), [pltpu.VMEM((ROWS, 384), F32)])
    stacked = sds((2, ROWS, WIDE), F32)
    term_outs = [sds((ROWS, WIDE), BF)] * 2
    term_scratch = pltpu.VMEM((2, ROWS, WIDE), BF)
    places_column = mask_places.reshape(2 * slots, 1)
    matmul_flops = 2 * 2 * ROWS * WIDE

    stream, qk, v, attended, attend_entered, keep, send = call(
        functools.partial(attend_kernel, nb),
        [stacked, sds((2 * ROWS, 2 * share), BF), sds((2 * ROWS, share), BF), sds((2 * ROWS, share), BF)]
        + [sds((2 * ROWS, WIDE), BF)]
        + term_outs,
        (sc, images, mask_places, vectors, in_biases, bias, *patch_quarters, *first_blocks),
        [weight_scratch(first_blocks), term_scratch, pltpu.VMEM((4, WIDE, quarter), BF)],
        matmul_flops * 2 * WIDE,
    )
    attend_own, attend_other = tensor_sum(keep, send)
    middle, pre, active, feed_entered, keep, send = call(
        functools.partial(feed_kernel, nb),
        [stacked, sds((2 * ROWS, WIDE), F32)] + [sds((2 * ROWS, WIDE), BF)] * 2 + term_outs,
        (sc, stream, attend_own, attend_other, vectors, in_biases, *second_blocks),
        [weight_scratch(second_blocks), term_scratch],
        matmul_flops * 2 * WIDE,
    )
    feed_own, feed_other = tensor_sum(keep, send)
    last, picked, logits, stats = call(
        functools.partial(logit_kernel, nb),
        [stacked, sds((2 * slots, WIDE), BF), sds((2 * slots, code_share), F32), sds((2 * slots, 128), F32)],
        (sc, middle, feed_own, feed_other, vectors, places_column, codes, logit_bias.reshape(1, -1), *code_blocks, *more_blocks),
        [weight_scratch(code_blocks), weight_scratch(more_blocks)],
        matmul_flops * 2 * WIDE,
    )
    all_stats = [stats] + [tp_permute(stats, k) for k in (1, 2, 3)]
    slot_outs = [sds((slots, WIDE), BF)] * 2
    grad_logits, logit_sums, loss, keep, send = call(
        functools.partial(loss_kernel, nb),
        [sds((2 * slots, code_share), BF), sds((1, code_share), F32), sds((1, 128), F32)] + slot_outs,
        (sc, *all_stats, logits, *code_blocks, *more_blocks),
        [weight_scratch(code_blocks), weight_scratch(more_blocks), pltpu.VMEM((2, slots, WIDE), BF)],
        matmul_flops * 2 * WIDE,
    )
    picked_own, picked_other = tensor_sum(keep, send)
    code_parts = []
    first = 0
    for g, wide in enumerate(CODE_PIECES):
        wide = wide * code_share // sum(CODE_PIECES)
        if g == 0 and dp == 8:
            parts = call(
                functools.partial(z_first_kernel, first, wide),
                [sds((2, WIDE // 8, wide), BF)] * 4,
                (sc, picked, grad_logits),
                [grad_scratch(WIDE, wide)],
                2 * 2 * slots * WIDE * wide,
            )
            code_parts.append(z_first_start(sc, parts))
            first += wide
            continue
        grads = call(
            functools.partial(code_grad_kernel, first, wide),
            grad_outs(1, WIDE, wide, dp),
            (sc, picked, grad_logits),
            [grad_scratch(WIDE, wide)],
            2 * 2 * slots * WIDE * wide,
        )
        first += wide
        code_parts.append(scatter_start(sc, grads))

    upstream, gated, grad_pre, feed_sums, keep, send = call(
        functools.partial(feed_back_kernel, nb),
        [stacked, sds((2 * ROWS, WIDE), BF), sds((2 * ROWS, WIDE), BF), sds((8, WIDE), F32)] + term_outs,
        (sc, picked_own, picked_other, places_column, last, feed_own, feed_other, vectors, pre, *second_blocks),
        [weight_scratch(second_blocks), term_scratch, pltpu.VMEM((2, slots, WIDE), BF)],
        matmul_flops * 2 * WIDE,
    )
    feed_in_own, feed_in_other = tensor_sum(keep, send)
    pair_scratch = [grad_scratch(WIDE, 2 * share)]
    feed_part = scatter_start(
        sc,
        call(
            feed_grad_kernel, grad_outs(4, WIDE, 2 * share, dp),
            (sc, feed_entered, grad_pre, gated, active),
            pair_scratch, 2 * matmul_flops * WIDE,
        ),
    )
    passed, gated, grad_qk, grad_v, attend_sums, table_sums, keep, send = call(
        functools.partial(attend_back_kernel, nb),
        [
            stacked, sds((2 * ROWS, WIDE), BF), sds((2 * ROWS, 2 * share), BF), sds((2 * ROWS, share), BF),
            sds((8, WIDE), F32), sds((heads, WIDE), F32),
        ]
        + term_outs,
        (sc, feed_in_own, feed_in_other, upstream, middle, attend_own, attend_other, vectors, qk, v, bias, *first_blocks),
        [
            weight_scratch(first_blocks), term_scratch, pltpu.VMEM((2 * ROWS, share), BF),
            pltpu.VMEM((ROWS, 384), F32), pltpu.VMEM((2, heads, ROWS, ROWS), BF),
        ],
        matmul_flops * 2 * WIDE,
    )
    attend_in_own, attend_in_other = tensor_sum(keep, send)
    first_grads = call(
        attend_grad_kernel, grad_outs(2, WIDE, 2 * share, dp),
        (sc, attend_entered, grad_qk, grad_v, gated, attended), pair_scratch, matmul_flops * WIDE,
    )
    small_rows = 15 + heads + -(-code_share // WIDE) + 1
    embed_outs = call(
        embed_back_kernel,
        [sds((small_rows, WIDE), F32)] + grad_outs(1, WIDE, quarter, dp),
        (
            sc, attend_in_own, attend_in_other, passed, stream, vectors, images, mask_places,
            feed_sums, attend_sums, table_sums, logit_sums, loss,
        ),
        [grad_scratch(WIDE, quarter), pltpu.VMEM((2, ROWS, WIDE), F32), pltpu.VMEM((4, 2, NPATCH, quarter), BF)],
        matmul_flops * WIDE,
    )
    late_part = late_start(sc, first_grads, embed_outs[1:])
    small_part = small_start(embed_outs[0])
    early, squares = sum_early(sc, [*code_parts, feed_part])
    first_shard, patch_shard, small, shares = sum_late(sc, squares, late_part, small_part, dp, tp)
    spread = lax.all_to_all(shares, ("dp", "tensor"), 0, 0)
    patch_shards = tensor_gather(patch_shard)
    step_number = step_count[0].astype(F32)
    fix = jnp.stack([1.0 - jnp.power(BETA_ONE, step_number), jnp.sqrt(1.0 - jnp.power(BETA_TWO, step_number))])

    def like(array):
        return sds(array.shape, F32)

    in_w, in_m = in_weights.transpose(0, 2, 1, 3), in_moments.transpose(0, 1, 3, 2, 4)
    in_master, in_state, out_master, out_state, patch_master, patch_state = call(
        adam_matrix_kernel,
        [like(a) for a in (in_w, in_m, out_weights, out_moments, patch_weight, patch_moments)],
        (
            sc, fix, spread, in_w, in_m, out_weights, out_moments, patch_weight, patch_moments,
            first_shard, early[-1], *patch_shards,
        ),
        [pltpu.VMEM((4,) + patch_shard.shape, F32)],
        scalars=2,
    )
    code_master, code_state = call(
        functools.partial(adam_code_kernel, len(code_parts)),
        [like(code_weight), like(code_moments)],
        (sc, fix, spread, code_weight, code_moments, *early[:-1]),
        scalars=2,
    )
    logit_row = logit_bias.reshape(1, -1)
    bias_w, bias_m = in_biases.transpose(1, 0, 2), bias_moments.transpose(0, 2, 1, 3)
    vec_m, table_m = vector_moments.transpose(1, 0, 2), table_moments.transpose(1, 0, 2)
    bias_master, bias_state, vec_master, vec_state, table_master, table_state, logit_master, logit_state, loss_value, grad_norm = call(
        adam_small_kernel,
        [like(a) for a in (bias_w, bias_m, vectors, vec_m, rel_table, table_m, logit_row, logit_moments)]
        + [sds((1,), F32)] * 2,
        (sc, fix, spread, small, bias_w, bias_m, vectors, vec_m, rel_table, table_m, logit_row, logit_moments),
        scalars=2,
        scalar_outs=2,
    )
    return (
        loss_value, grad_norm,
        in_master.transpose(0, 2, 1, 3), in_state.transpose(0, 1, 3, 2, 4),
        out_master, out_state, patch_master, patch_state, code_master, code_state,
        bias_master.transpose(1, 0, 2), bias_state.transpose(0, 2, 1, 3),
        vec_master, vec_state.transpose(1, 0, 2), table_master, table_state.transpose(1, 0, 2),
        logit_master.reshape(-1), logit_state,
    )


def solution(mesh):
    in_specs = (
        P("dp", None, None),
        P("dp", None),
        P(),
        P("dp", None),
        P(),
        P(None, "dp", None, "tensor"),
        P(None, None, "dp", None, "tensor"),
        P(None, None, "tensor", "dp"),
        P(None, None, None, "tensor", "dp"),
        P("dp", None),
        P(None, "dp", None),
        P("dp", "tensor"),
        P(None, "dp", "tensor"),
        P(None, None, "tensor"),
        P(None, None, None, "tensor"),
        P(),
        P(),
        P("tensor", None),
        P(None, "tensor", None),
        P("tensor"),
        P(None, "tensor"),
    )
    out_specs = (P(), P()) + in_specs[5:]

    return jax.shard_map(local, mesh=mesh, in_specs=in_specs, out_specs=out_specs, check_vma=False)
```
